32 devices in a mesh: row: 8 (over y, x, core), blk: 4 (over z).
Axes of the slice: x: 2, y: 2, z: 4, core: 2. Of those that a mesh axis runs over, the one named last changes fastest.
Arguments:
- values: bfloat16 [512, 16, 256, 256], P('row', 'blk'), may hold values from -6 to 6
- scales: bfloat16 [512, 16], P('row', 'blk'), may hold values from 0.0049743652 to 0.049804688
- pattern: int32 [512, 16], P('row', 'blk'), may hold values from 0 to 2047, as said below
- omega: bfloat16 [2048, 256, 128], P(('row', 'blk')), may hold values from -6 to 6
Outputs:
- basis: float32 [2048, 256, 128], P(('row', 'blk'))
- upper: float32 [128, 128], replicated
The draws below stay inside these ranges and needn't reach their ends.
Inputs may be any that keep to these rules, and one draw needn't show every extreme that they name: `pattern`: A block-row of group g = r // 64 has all its column blocks in g * 256 to (g + 1) * 256 - 1. Among the 256 blocks of one device (its block-rows and its positions), at most 64 lie in one aligned run of 64 column blocks, and some run holds exactly 64.
All inputs are finite; a program needn't handle non-finite values.
Results may differ from the reference program's by a relative error of at most 0.0003.
Values may be sent and summed in bfloat16 or wider, within the bound.
A program may use at most 192 MiB of HBM per device.

```python
import math
import jax
import jax.numpy as jnp
from jax import lax

BS = 256
P_SIZE = 128
NCB = 2048
K = 16
RB = 64
KDEV = 4
MB = 512
CAP = 64


def draw_pattern(key, part):
    block_count = RB * KDEV
    cycle_size = K // KDEV
    row_groups = MB // RB
    col_per_dev = NCB // (row_groups * cycle_size)

    def one_device(index):
        device_key = jax.random.fold_in(key, index)
        key_hot, key_perm, key_local = jax.random.split(device_key, 3)
        hot_owner = jax.random.randint(key_hot, (), 0, cycle_size)
        slots = jnp.arange(block_count)
        others = (hot_owner + 1 + (slots - CAP) % (cycle_size - 1)) % cycle_size
        owner_list = jnp.where(slots < CAP, hot_owner, others)
        owner_list = jax.random.permutation(key_perm, owner_list)
        local_list = jax.random.randint(key_local, (block_count,), 0, col_per_dev)
        group_base = index // cycle_size * col_per_dev * cycle_size
        return (group_base + owner_list * col_per_dev + local_list).reshape(RB, KDEV)
    tables = jax.vmap(one_device)(jnp.arange(row_groups * cycle_size))
    return tables.reshape(row_groups, cycle_size, RB, KDEV).transpose(0, 2, 1, 3).reshape(MB, K).astype(jnp.int32)


def levels(own_key, shape, cuts, smallest, largest):
    def one(dim, parts):
        steps = jax.random.uniform(jax.random.fold_in(jax.random.fold_in(own_key, 6), dim), (parts,), jnp.float32, smallest / len(cuts), largest / len(cuts))
        return jnp.repeat(jnp.exp(steps), shape[dim] // parts).reshape((-1,) + (1,) * (len(shape) - dim - 1))

    gain = one(*cuts[0])
    for cut in cuts[1:]:
        gain = gain * one(*cut)
    return gain


def normal_values(stream_key, shape, width, reach, pieces=(), dtype=jnp.bfloat16):
    result = width * jax.random.normal(stream_key, shape, jnp.float32)
    if pieces:
        result = result * levels(stream_key, shape, pieces, -0.22, 0.18)
    return jnp.clip(result, -reach, reach).astype(dtype)


def setup_inputs(seed: int = 0) -> dict:
    key_of = jax.random.split(jax.random.key(seed), 5)
    return {
        "values": normal_values(key_of[0], (MB, K, BS, BS), 1.0, 6.0, ((0, 8), (1, 4))),
        "scales": jnp.clip(jnp.exp(math.log(0.049804688) - 2.3038113 * jax.random.uniform(key_of[1], (MB, K), jnp.float32) ** levels(key_of[1], (MB, K), ((0, 8), (1, 4)), -0.2, 0.2)), 0.0049743652, 0.049804688).astype(jnp.bfloat16),
        "pattern": draw_pattern(jax.random.fold_in(key_of[4], 71), 0),
        "omega": normal_values(key_of[3], (NCB, BS, P_SIZE), 1.0, 6.0, ((0, 32),)),
    }


def reference(values, scales, pattern, omega):
    weights = scales.astype(jnp.float32)

    def row_product(item_tuple):
        blocks, scale_row, col_blocks = item_tuple
        picked = jnp.take(omega, col_blocks, axis=0).astype(jnp.float32)
        products = jnp.einsum('kij,kjc->kic', blocks.astype(jnp.float32), picked) * scale_row[:, None, None]
        partial_value = jnp.sum(products.reshape(K // KDEV, KDEV, BS, P_SIZE), axis=1)
        return jnp.sum(partial_value, axis=0)
    rowvec = lax.map(row_product, (values, weights, pattern))

    def add_row(running_sum, item_tuple):
        blocks, scale_row, col_blocks, row_vecs = item_tuple
        row_high = lax.optimization_barrier(row_vecs.astype(jnp.bfloat16))
        row_low = (row_vecs - row_high.astype(jnp.float32)).astype(jnp.bfloat16)
        blocks_wide = blocks.astype(jnp.float32)
        high_part = jnp.einsum('kji,jc->kic', blocks_wide, row_high.astype(jnp.float32))
        low_part = jnp.einsum('kji,jc->kic', blocks_wide, row_low.astype(jnp.float32))
        contrib = (high_part + low_part) * scale_row[:, None, None]
        return (running_sum.at[col_blocks].add(contrib), None)
    start_sum = jnp.zeros((NCB, BS, P_SIZE), jnp.float32)
    colsum, unused = lax.scan(add_row, start_sum, (values, weights, pattern, rowvec))
    flat_sum = colsum.reshape(NCB * BS, P_SIZE)
    gram = jnp.dot(flat_sum.T, flat_sum, precision=lax.Precision.HIGHEST) / (NCB * BS)
    lower_factor = jnp.linalg.cholesky(gram)
    solved = jax.scipy.linalg.solve_triangular(lower_factor, flat_sum.T, lower=True)
    return (solved.T.reshape(NCB, BS, P_SIZE), lower_factor.T)
```

```python
import functools

import jax
import jax.numpy as jnp
from jax import lax
from jax.experimental import pallas as pl
from jax.experimental.pallas import tpu as pltpu
from jax.sharding import PartitionSpec as P

MESH = pl.DeviceIdType.MESH
LEVELS = 32767.0
TINY = 1e-30
HOP = 2
ANY = pl.BlockSpec(memory_space=pl.ANY)
SMEM = pl.BlockSpec(memory_space=pltpu.SMEM)


def divisor(n, most):
    return max(d for d in range(1, most + 1) if n % d == 0)


def diagonal(height, width):
    shape = (height, width)
    return lax.broadcasted_iota(jnp.int32, shape, 0) == lax.broadcasted_iota(jnp.int32, shape, 1)


def encode(x, eye):
    peak = jnp.max(jnp.abs(x), axis=2, keepdims=True)
    live = peak > TINY
    inverse = jnp.where(live, LEVELS / jnp.where(live, peak, 1.0), 0.0)
    code = jnp.round(x * inverse).astype(jnp.int32).astype(jnp.int16)
    step = jnp.sum(jnp.where(eye[None], peak * (1.0 / LEVELS), 0.0), axis=1, keepdims=True)
    return code, step


def decode(code, step, eye):
    column = jnp.sum(jnp.where(eye[None], step, 0.0), axis=2, keepdims=True)
    return code.astype(jnp.int32).astype(jnp.float32) * column


def greet(me, n):
    barrier = pltpu.get_barrier_semaphore()

    @pl.when(me > 0)
    def _():
        pl.semaphore_signal(barrier, inc=1, device_id={"blk": me - 1}, device_id_type=MESH)

    @pl.when(me < n - 1)
    def _():
        pl.semaphore_signal(barrier, inc=1, device_id={"blk": me + 1}, device_id_type=MESH)

    peers = jnp.where(me > 0, 1, 0) + jnp.where(me < n - 1, 1, 0)
    pl.semaphore_wait(barrier, peers)


def gather_steps(me, n, own_ref, slab_ref, send_sem, recv_sem):
    blocks = own_ref.shape[0]
    pieces = send_sem.shape[2]
    size = blocks // pieces

    def copy(way, t, c, owner):
        src = slab_ref.at[pl.ds(owner * blocks + c * size, size)]
        return pltpu.make_async_remote_copy(
            src_ref=src,
            dst_ref=src,
            send_sem=send_sem.at[way, t, c],
            recv_sem=recv_sem.at[way, t, c],
            device_id={"blk": me + 1 - 2 * way},
            device_id_type=MESH,
        )

    def first(way, c):
        return pltpu.make_async_remote_copy(
            src_ref=own_ref.at[pl.ds(c * size, size)],
            dst_ref=slab_ref.at[pl.ds(me * blocks + c * size, size)],
            send_sem=send_sem.at[way, 0, c],
            recv_sem=recv_sem.at[way, 0, c],
            device_id={"blk": me + 1 - 2 * way},
            device_id_type=MESH,
        )

    def has(way, t):
        behind = me if way == 0 else n - 1 - me
        return behind >= t

    def goes(way):
        return me < n - 1 if way == 0 else me > 0

    def owner_of(way, t):
        return me - t if way == 0 else me + t

    def step(v):
        t = v // pieces
        c = v % pieces
        for way in (0, 1):

            @pl.when((t == 0) & goes(way))
            def _(way=way):
                first(way, c).start()

            @pl.when((t > 0) & has(way, t))
            def _(way=way):
                copy(way, t - 1, c, owner_of(way, t)).wait_recv()

            @pl.when((t > 0) & (t < n - 1) & has(way, t) & goes(way))
            def _(way=way):
                copy(way, t, c, owner_of(way, t)).start()

    def finish():
        @pl.loop(0, (n - 1) * pieces)
        def _(v):
            t = v // pieces
            c = v % pieces
            for way in (0, 1):

                @pl.when(has(way, t) & goes(way))
                def _(way=way):
                    copy(way, t, c, me).wait_send()

    return step, n * pieces, finish


def gather(own, n, part):
    blocks = own.shape[0]
    pieces = divisor(blocks, 8)

    def body(own_ref, slab_ref, send_sem, recv_sem):
        me = lax.axis_index("blk")
        greet(me, n)
        step, steps, finish = gather_steps(me, n, own_ref, slab_ref, send_sem, recv_sem)
        pl.loop(0, steps)(step)
        finish()

    return pl.pallas_call(
        body,
        out_shape=jax.ShapeDtypeStruct((n * blocks,) + own.shape[1:], own.dtype),
        in_specs=[ANY],
        out_specs=ANY,
        scratch_shapes=[pltpu.SemaphoreType.DMA((2, n - 1, pieces))] * 2,
        compiler_params=pltpu.CompilerParams(collective_id=1 + part, has_side_effects=True),
        name=f"gather_{part}",
    )(own)


def products(values, own, slab, cols, weights, prev, last, n, part):
    rows, per, side, _ = values.shape
    blocks, wide, _ = own.shape
    lanes = 128
    items = rows * per
    columns = n * blocks
    batch = divisor(rows, 4)
    pieces = rows // batch
    lag = HOP * (n - 1)
    slots = lag + 2
    out_batch = divisor(columns, 8)

    def body(
        cols_ref, weights_ref, prev_ref, last_ref, values_ref, own_ref, slab_ref, z_ref,
        slab, ring, part_ref, in_code, in_step, out_code, out_step, sums, stage,
        slab_sem, ring_sem, stage_sem, send_sem, recv_sem,
    ):
        me = lax.axis_index("blk")
        eye = diagonal(wide, lanes)

        def load(c):
            slot = c % slots
            return pltpu.make_async_copy(
                values_ref.at[pl.ds(c * batch, batch)], ring.at[slot], ring_sem.at[slot]
            )

        def shard(d, src):
            return pltpu.make_async_copy(src, slab.at[pl.ds(d * blocks, blocks)], slab_sem.at[d])

        load(0).start()
        for d in range(n):

            @pl.when(me == d)
            def _(d=d):
                shard(d, own_ref).start()

            @pl.when(me != d)
            def _(d=d):
                shard(d, slab_ref.at[pl.ds(d * blocks, blocks)]).start()

        greet(me, n)
        sums[items] = jnp.zeros((wide, side), jnp.float32)

        @pl.when(me == 0)
        def _():
            in_step[0] = jnp.zeros((rows, 1, lanes), jnp.float32)

        @pl.when(me == n - 1)
        def _():
            in_step[1] = jnp.zeros((rows, 1, lanes), jnp.float32)

        for d in range(n):
            shard(d, own_ref).wait()

        def copies(way, c):
            to = {"blk": me + 1 - 2 * way}
            at = pl.ds(c * batch, batch)
            return [
                pltpu.make_async_remote_copy(
                    src_ref=src.at[way, at],
                    dst_ref=dst.at[way, at],
                    send_sem=send_sem.at[way, kind, c],
                    recv_sem=recv_sem.at[way, kind, c],
                    device_id=to,
                    device_id_type=MESH,
                )
                for kind, (src, dst) in enumerate(((out_code, in_code), (out_step, in_step)))
            ]

        def incoming(way, c):
            at = pl.ds(c * batch, batch)
            return decode(in_code[way, at], in_step[way, at], eye)

        def relay(way, c, has, goes):
            @pl.when((c >= 0) & (c < pieces) & has)
            def _():
                for one in copies(way, c):
                    one.wait_recv()

            @pl.when((c >= 0) & (c < pieces) & goes)
            def _():
                at = pl.ds(c * batch, batch)
                code, step = encode(part_ref[at] + incoming(way, c), eye)
                out_code[way, at] = code
                out_step[way, at] = step
                for one in copies(way, c):
                    one.start()

        @pl.loop(0, pieces + lag)
        def _(s):
            @pl.when(s + 1 < pieces)
            def _():
                load(s + 1).start()

            @pl.when(s < pieces)
            def _():
                load(s).wait()
                for r in range(batch):
                    total = None
                    for k in range(per):
                        at = (s * batch + r) * per + k
                        term = weights_ref[at] * lax.dot_general(
                            slab[cols_ref[at]],
                            ring[s % slots, r, k],
                            (((1,), (1,)), ((), ())),
                            preferred_element_type=jnp.float32,
                        )
                        total = term if total is None else total + term
                    part_ref[s * batch + r] = total

            relay(0, s - HOP * me, me > 0, me < n - 1)
            relay(1, s - HOP * (n - 1 - me), me < n - 1, me > 0)
            c = s - lag

            @pl.when(c >= 0)
            def _():
                total = part_ref[pl.ds(c * batch, batch)] + incoming(0, c) + incoming(1, c)
                high = total.astype(jnp.bfloat16)
                low = (total - high.astype(jnp.float32)).astype(jnp.bfloat16)
                for r in range(batch):
                    both = jnp.concatenate([high[r], low[r]], axis=0)
                    for k in range(per):
                        at = (c * batch + r) * per + k
                        pair = lax.dot_general(
                            both,
                            ring[c % slots, r, k],
                            (((1,), (0,)), ((), ())),
                            preferred_element_type=jnp.float32,
                        )
                        term = weights_ref[at] * (pair[:wide] + pair[wide:])
                        sums[at] = term + sums[prev_ref[at]]

        @pl.loop(0, pieces)
        def _(c):
            @pl.when(me < n - 1)
            def _():
                for one in copies(0, c):
                    one.wait_send()

            @pl.when(me > 0)
            def _():
                for one in copies(1, c):
                    one.wait_send()

        def store(i):
            return pltpu.make_async_copy(
                stage.at[i % 2], z_ref.at[pl.ds(i * out_batch, out_batch)], stage_sem.at[i % 2]
            )

        count = columns // out_batch

        @pl.loop(0, count)
        def _(i):
            @pl.when(i >= 2)
            def _():
                store(i - 2).wait()

            for u in range(out_batch):
                stage[i % 2, u] = sums[last_ref[i * out_batch + u]]
            store(i).start()

        for i in range(max(count - 2, 0), count):
            store(i).wait()

    f32 = jnp.float32
    return pl.pallas_call(
        body,
        out_shape=jax.ShapeDtypeStruct((columns, wide, side), f32),
        in_specs=[SMEM] * 4 + [ANY] * 3,
        out_specs=ANY,
        scratch_shapes=[
            pltpu.VMEM((columns, wide, side), own.dtype),
            pltpu.VMEM((slots, batch, per, side, side), values.dtype),
            pltpu.VMEM((rows, wide, side), f32),
            pltpu.VMEM((2, rows, wide, side), jnp.int16),
            pltpu.VMEM((2, rows, 1, lanes), f32),
            pltpu.VMEM((2, rows, wide, side), jnp.int16),
            pltpu.VMEM((2, rows, 1, lanes), f32),
            pltpu.VMEM((items + 1, wide, side), f32),
            pltpu.VMEM((2, out_batch, wide, side), f32),
            pltpu.SemaphoreType.DMA((n,)),
            pltpu.SemaphoreType.DMA((slots,)),
            pltpu.SemaphoreType.DMA((2,)),
            pltpu.SemaphoreType.DMA((2, 2, pieces)),
            pltpu.SemaphoreType.DMA((2, 2, pieces)),
        ],
        compiler_params=pltpu.CompilerParams(
            collective_id=8 + part, has_side_effects=True, vmem_limit_bytes=62 << 20
        ),
        name=f"products_{part}",
    )(cols, weights, prev, last, values, own, slab)


def scatter(z, n, part, own=None):
    columns, wide, side = z.shape
    lanes = 128
    blocks = columns // n
    pieces = divisor(blocks, 8)
    size = blocks // pieces
    reach = (n - 1) * pieces
    total_steps = max(reach + HOP, pieces + HOP * (n - 1))
    fused = own is not None
    if fused:
        total_steps = max(total_steps, n * pieces)

    def body(*refs):
        if fused:
            z_ref, own_ref, out_ref, slab_ref = refs[:4]
            refs = refs[4:]
            gather_send, gather_recv = refs[-2:]
        else:
            z_ref, out_ref = refs[:2]
            refs = refs[2:]
        (zs, mine, in_code, in_step, out_code, out_step, z_sem, mine_sem, send_sem, recv_sem) = refs[:10]
        me = lax.axis_index("blk")
        eye = diagonal(wide, lanes)

        def spot(way, u):
            d = n - 1 - u // pieces if way == 0 else u // pieces
            return pl.ds(d * blocks + u % pieces * size, size)

        def load(way, u):
            at = spot(way, u)
            return pltpu.make_async_copy(z_ref.at[at], zs.at[at], z_sem.at[way, u])

        mine_copy = pltpu.make_async_copy(z_ref.at[pl.ds(me * blocks, blocks)], mine, mine_sem)
        far = ((n - 1 - me) * pieces, me * pieces)

        @pl.loop(0, reach)
        def _(u):
            for way in (0, 1):

                @pl.when(u < far[way])
                def _(way=way):
                    load(way, u).start()

        mine_copy.start()
        greet(me, n)

        def copies(way, u):
            here = pl.ds(u * size, size)
            to = {"blk": me + 1 - 2 * way}
            return [
                pltpu.make_async_remote_copy(
                    src_ref=src.at[way, here],
                    dst_ref=dst.at[way, here],
                    send_sem=send_sem.at[way, kind, u],
                    recv_sem=recv_sem.at[way, kind, u],
                    device_id=to,
                    device_id_type=MESH,
                )
                for kind, (src, dst) in enumerate(((out_code, in_code), (out_step, in_step)))
            ]

        def incoming(way, u):
            here = pl.ds(u * size, size)
            return decode(in_code[way, here], in_step[way, here], eye)

        def push(way, u, value):
            here = pl.ds(u * size, size)
            code, step = encode(value, eye)
            out_code[way, here] = code
            out_step[way, here] = step
            for one in copies(way, u):
                one.start()

        if fused:
            step, steps, finish = gather_steps(me, n, own_ref, slab_ref, gather_send, gather_recv)

        mine_copy.wait()

        @pl.loop(0, total_steps)
        def _(s):
            if fused:

                @pl.when(s < steps)
                def _():
                    step(s)

            for way in (0, 1):
                behind = me if way == 0 else n - 1 - me
                u = s - HOP * behind
                inside = (u >= 0) & (u < far[way])

                @pl.when(inside)
                def _(way=way, u=u):
                    load(way, u).wait()

                @pl.when(inside & (behind == 0))
                def _(way=way, u=u):
                    push(way, u, zs[spot(way, u)])

                @pl.when(inside & (behind > 0))
                def _(way=way, u=u):
                    for one in copies(way, u):
                        one.wait_recv()
                    push(way, u, zs[spot(way, u)] + incoming(way, u))

                @pl.when((behind > 0) & (u >= far[way]) & (u < far[way] + pieces))
                def _(way=way, u=u):
                    for one in copies(way, u):
                        one.wait_recv()
                    at = pl.ds((u - far[way]) * size, size)
                    mine[at] = mine[at] + incoming(way, u)

        result = pltpu.make_async_copy(mine, out_ref, mine_sem)
        result.start()

        @pl.loop(0, reach)
        def _(u):
            for way in (0, 1):

                @pl.when(u < far[way])
                def _(way=way):
                    for one in copies(way, u):
                        one.wait_send()

        if fused:
            finish()
        result.wait()

    f32 = jnp.float32
    scratch = [
        pltpu.VMEM((columns, wide, side), f32),
        pltpu.VMEM((blocks, wide, side), f32),
        pltpu.VMEM((2, reach * size, wide, side), jnp.int16),
        pltpu.VMEM((2, reach * size, 1, lanes), f32),
        pltpu.VMEM((2, reach * size, wide, side), jnp.int16),
        pltpu.VMEM((2, reach * size, 1, lanes), f32),
        pltpu.SemaphoreType.DMA((2, reach)),
        pltpu.SemaphoreType.DMA(()),
        pltpu.SemaphoreType.DMA((2, 2, reach)),
        pltpu.SemaphoreType.DMA((2, 2, reach)),
    ]
    out_shape = [jax.ShapeDtypeStruct((blocks, wide, side), f32)]
    args = [z]
    if fused:
        args.append(own)
        out_shape.append(jax.ShapeDtypeStruct((columns,) + own.shape[1:], own.dtype))
        scratch += [pltpu.SemaphoreType.DMA((2, n - 1, divisor(blocks, 8)))] * 2
    return pl.pallas_call(
        body,
        out_shape=out_shape,
        in_specs=[ANY] * len(args),
        out_specs=[ANY] * len(out_shape),
        scratch_shapes=scratch,
        compiler_params=pltpu.CompilerParams(
            collective_id=16 + part, has_side_effects=True, vmem_limit_bytes=62 << 20
        ),
        name=f"scatter_{part}",
    )(*args)


def all_sum(x, axis):
    n = lax.axis_size(axis)
    if n & (n - 1):
        return lax.psum(x, axis)
    bit = 1
    while bit < n:
        x = x + lax.ppermute(x, axis, [(i, i ^ bit) for i in range(n)])
        bit *= 2
    return x


def gram_of(z):
    blocks, width, side = z.shape
    batch = divisor(blocks, 8)

    def body(z_ref, out_ref):
        @pl.when(pl.program_id(0) == 0)
        def _():
            out_ref[...] = jnp.zeros_like(out_ref)

        for b in range(batch):
            out_ref[...] += lax.dot_general(
                z_ref[b],
                z_ref[b],
                (((1,), (1,)), ((), ())),
                precision=lax.Precision.HIGHEST,
                preferred_element_type=jnp.float32,
            )

    return pl.pallas_call(
        body,
        out_shape=jax.ShapeDtypeStruct((width, width), jnp.float32),
        grid=(blocks // batch,),
        in_specs=[pl.BlockSpec((batch, width, side), lambda i: (i, 0, 0))],
        out_specs=pl.BlockSpec((width, width), lambda i: (0, 0)),
        name="gram",
    )(z)


def solve(z, inverse):
    blocks, width, side = z.shape
    batch = divisor(blocks, 8)

    def body(z_ref, inverse_ref, out_ref):
        for b in range(batch):
            out_ref[b] = lax.dot_general(
                z_ref[b],
                inverse_ref[...],
                (((0,), (1,)), ((), ())),
                precision=lax.Precision.HIGHEST,
                preferred_element_type=jnp.float32,
            )

    return pl.pallas_call(
        body,
        out_shape=jax.ShapeDtypeStruct((blocks, side, width), jnp.float32),
        grid=(blocks // batch,),
        in_specs=[
            pl.BlockSpec((batch, width, side), lambda i: (i, 0, 0)),
            pl.BlockSpec((width, width), lambda i: (0, 0)),
        ],
        out_specs=pl.BlockSpec((batch, side, width), lambda i: (i, 0, 0)),
        name="solve",
    )(z, inverse)


def local(values, scales, pattern, omega):
    rows, per = pattern.shape
    blocks, side, width = omega.shape
    n = lax.axis_size("blk")
    items = rows * per
    columns = blocks * n
    cols = pattern.reshape(-1) - lax.axis_index("row") * columns
    weights = scales.astype(jnp.float32).reshape(-1)
    slot = jnp.arange(items)
    same = cols[:, None] == cols[None, :]
    prev = jnp.max(jnp.where(same & (slot[None, :] < slot[:, None]), slot[None, :], -1), axis=1)
    prev = jnp.where(prev < 0, items, prev)
    hits = jnp.arange(columns)[:, None] == cols[None, :]
    last = jnp.max(jnp.where(hits, slot[None, :], -1), axis=1)
    last = jnp.where(last < 0, items, last)

    parts = 2
    wide = width // parts
    turned = jnp.transpose(omega, (0, 2, 1)).reshape(blocks, parts, wide, side)
    own = [turned[:, p] for p in range(parts)]
    slab = gather(own[0], n, 0)
    sums = []
    for p in range(parts):
        z = products(values, own[p], slab, cols, weights, prev, last, n, p)
        if p + 1 < parts:
            piece, slab = scatter(z, n, p, own[p + 1])
        else:
            (piece,) = scatter(z, n, p)
        sums.append(piece)
    flat = jnp.concatenate(sums, axis=1)

    total_rows = columns * side * lax.axis_size("row")
    gram = all_sum(all_sum(gram_of(flat), "row"), "blk") / total_rows
    lower = jnp.linalg.cholesky(gram)
    inverse = jax.scipy.linalg.solve_triangular(lower, jnp.eye(width, dtype=jnp.float32), lower=True)
    return solve(flat, inverse), lower.T


def solution(mesh):
    return jax.shard_map(
        local,
        mesh=mesh,
        in_specs=(
            P("row", "blk", None, None),
            P("row", "blk"),
            P("row", "blk"),
            P(("row", "blk"), None, None),
        ),
        out_specs=(P(("row", "blk"), None, None), P()),
        check_vma=False,
    )
```

```python
import math

import jax
import jax.numpy as jnp
from jax import lax
from jax.experimental import pallas as pl
from jax.experimental.pallas import tpu as pltpu
from jax.sharding import PartitionSpec as P

MESH = pl.DeviceIdType.MESH
LEVELS = 32767.0
TINY = 1e-30
HOP = 2
ANY = pl.BlockSpec(memory_space=pl.ANY)
SMEM = pl.BlockSpec(memory_space=pltpu.SMEM)


def divisor(n, most):
    return max(d for d in range(1, most + 1) if n % d == 0)


def diagonal(height, width):
    shape = (height, width)
    return lax.broadcasted_iota(jnp.int32, shape, 0) == lax.broadcasted_iota(jnp.int32, shape, 1)


def encode(x, eye):
    peak = jnp.max(jnp.abs(x), axis=2, keepdims=True)
    live = peak > TINY
    inverse = jnp.where(live, LEVELS / jnp.where(live, peak, 1.0), 0.0)
    code = jnp.round(x * inverse).astype(jnp.int32).astype(jnp.int16)
    step = jnp.sum(jnp.where(eye[None], peak * (1.0 / LEVELS), 0.0), axis=1, keepdims=True)
    return code, step


def decode(code, step, eye):
    column = jnp.sum(jnp.where(eye[None], step, 0.0), axis=2, keepdims=True)
    return code.astype(jnp.int32).astype(jnp.float32) * column


def greet(me, n):
    barrier = pltpu.get_barrier_semaphore()

    @pl.when(me > 0)
    def _():
        pl.semaphore_signal(barrier, inc=1, device_id={"blk": me - 1}, device_id_type=MESH)

    @pl.when(me < n - 1)
    def _():
        pl.semaphore_signal(barrier, inc=1, device_id={"blk": me + 1}, device_id_type=MESH)

    peers = jnp.where(me > 0, 1, 0) + jnp.where(me < n - 1, 1, 0)
    pl.semaphore_wait(barrier, peers)


def gather_steps(me, n, base, count, size, own_ref, slab_ref, send_sem, recv_sem):
    blocks = own_ref.shape[0]
    pieces = count // size

    def copy(way, t, c, owner):
        here = slab_ref.at[pl.ds(owner * blocks + base + c * size, size)]
        return pltpu.make_async_remote_copy(
            src_ref=here,
            dst_ref=here,
            send_sem=send_sem.at[way, t, c],
            recv_sem=recv_sem.at[way, t, c],
            device_id={"blk": me + 1 - 2 * way},
            device_id_type=MESH,
        )

    def first(way, c):
        return pltpu.make_async_remote_copy(
            src_ref=own_ref.at[pl.ds(base + c * size, size)],
            dst_ref=slab_ref.at[pl.ds(me * blocks + base + c * size, size)],
            send_sem=send_sem.at[way, 0, c],
            recv_sem=recv_sem.at[way, 0, c],
            device_id={"blk": me + 1 - 2 * way},
            device_id_type=MESH,
        )

    def has(way, t):
        behind = me if way == 0 else n - 1 - me
        return behind >= t

    def goes(way):
        return me < n - 1 if way == 0 else me > 0

    def owner_of(way, t):
        return me - t if way == 0 else me + t

    def step(v):
        t = v // pieces
        c = v % pieces
        for way in (0, 1):

            @pl.when((t == 0) & goes(way))
            def _(way=way):
                first(way, c).start()

            @pl.when((t > 0) & has(way, t))
            def _(way=way):
                copy(way, t - 1, c, owner_of(way, t)).wait_recv()

            @pl.when((t > 0) & (t < n - 1) & has(way, t) & goes(way))
            def _(way=way):
                copy(way, t, c, owner_of(way, t)).start()

    def finish():
        @pl.loop(0, (n - 1) * pieces)
        def _(v):
            t = v // pieces
            c = v % pieces
            for way in (0, 1):

                @pl.when(has(way, t) & goes(way))
                def _(way=way):
                    copy(way, t, c, me).wait_send()

    return step, n * pieces, finish


def gather_sems(n, count, size):
    return [pltpu.SemaphoreType.DMA((2, n - 1, count // size))] * 2


def gather(own, n):
    blocks = own.shape[0]
    size = divisor(blocks, 4)

    def body(own_ref, slab_ref, *sems):
        me = lax.axis_index("blk")
        greet(me, n)
        step, steps, finish = gather_steps(me, n, 0, blocks, size, own_ref, slab_ref, *sems)
        pl.loop(0, steps)(step)
        finish()

    return pl.pallas_call(
        body,
        out_shape=jax.ShapeDtypeStruct((n * blocks,) + own.shape[1:], own.dtype),
        in_specs=[ANY],
        out_specs=ANY,
        scratch_shapes=gather_sems(n, blocks, size),
        compiler_params=pltpu.CompilerParams(collective_id=1, has_side_effects=True),
        name="gather",
    )(own)


def reduce_scratch(n, count, size, wide, side, lanes):
    far = (n - 1) * count
    sems = pltpu.SemaphoreType.DMA((2, 2, far // size))
    code = pltpu.VMEM((2, far, wide, side), jnp.int16)
    step = pltpu.VMEM((2, far, 1, lanes), jnp.float32)
    return [code, step, code, step, sems, sems]


def reduce_steps(me, n, count, size, eye, read, total, base, scratch, beside):
    in_code, in_step, out_code, out_step, send_sem, recv_sem = scratch
    pieces = count // size
    reach = (n - 1) * pieces
    far = ((n - 1 - me) * pieces, me * pieces)
    hop = max(pieces, HOP) if beside else HOP
    start = pieces if beside else 0

    def copies(way, u):
        here = pl.ds(u * size, size)
        to = {"blk": me + 1 - 2 * way}
        return [
            pltpu.make_async_remote_copy(
                src_ref=src.at[way, here],
                dst_ref=dst.at[way, here],
                send_sem=send_sem.at[way, kind, u],
                recv_sem=recv_sem.at[way, kind, u],
                device_id=to,
                device_id_type=MESH,
            )
            for kind, (src, dst) in enumerate(((out_code, in_code), (out_step, in_step)))
        ]

    def incoming(way, u):
        here = pl.ds(u * size, size)
        return decode(in_code[way, here], in_step[way, here], eye)

    def push(way, u, value):
        here = pl.ds(u * size, size)
        code, step = encode(value, eye)
        out_code[way, here] = code
        out_step[way, here] = step
        for one in copies(way, u):
            one.start()

    def source(way, u):
        d = n - 1 - u // pieces if way == 0 else u // pieces
        return read(d, u % pieces)

    def step(s):
        for way in (0, 1):
            behind = me if way == 0 else n - 1 - me
            u = s - start - hop * behind
            inside = (u >= 0) & (u < far[way])

            @pl.when(inside & (behind == 0))
            def _(way=way, u=u):
                push(way, u, source(way, u))

            @pl.when(inside & (behind > 0))
            def _(way=way, u=u):
                for one in copies(way, u):
                    one.wait_recv()
                push(way, u, source(way, u) + incoming(way, u))

            @pl.when((behind > 0) & (u >= far[way]) & (u < far[way] + pieces))
            def _(way=way, u=u):
                for one in copies(way, u):
                    one.wait_recv()
                at = pl.ds(base + (u - far[way]) * size, size)
                total[at] = total[at] + incoming(way, u)

    def finish():
        @pl.loop(0, reach)
        def _(u):
            for way in (0, 1):

                @pl.when(u < far[way])
                def _(way=way):
                    for one in copies(way, u):
                        one.wait_send()

    return step, start + max([reach] + [hop * b + (n - b) * pieces for b in range(1, n)]), finish


def stage(part, values, own, slab, tables, n, following=None, rest=None):
    rows, per, side, _ = values.shape
    blocks, wide, _ = own.shape
    lanes = 128
    items = rows * per
    columns = n * blocks
    batch = divisor(rows, 4)
    pieces = rows // batch
    lag = HOP * (n - 1)
    slots = lag + 2
    half = blocks // 2
    late = blocks - half
    now = half if following is not None else blocks
    now_size = divisor(now, 4 if following is not None else 8)
    late_size = divisor(late, 4)
    gather_size = divisor(half, 4)
    f32 = jnp.float32

    args = dict(zip(("cols", "weights", "prev", "last"), tables))
    args.update(values=values, own=own, slab=slab)
    specs = [SMEM] * 4 + [ANY] * 3
    cuts = [(0, half)] + ([(half, blocks)] if following is None else [])
    outs = {
        f"piece{i}": jax.ShapeDtypeStruct((b - a, wide, side), f32) for i, (a, b) in enumerate(cuts)
    }
    scratch = dict(
        held=pltpu.VMEM((columns, wide, side), own.dtype),
        ring=pltpu.VMEM((slots, batch, per, side, side), values.dtype),
        part=pltpu.VMEM((rows, wide, side), f32),
        in_code=pltpu.VMEM((2, rows, wide, side), jnp.int16),
        in_step=pltpu.VMEM((2, rows, 1, lanes), f32),
        out_code=pltpu.VMEM((2, rows, wide, side), jnp.int16),
        out_step=pltpu.VMEM((2, rows, 1, lanes), f32),
        sums=pltpu.VMEM((items + 1, wide, side), f32),
        mine=pltpu.VMEM((now, wide, side), f32),
        held_sem=pltpu.SemaphoreType.DMA((n,)),
        ring_sem=pltpu.SemaphoreType.DMA((slots,)),
        send_sem=pltpu.SemaphoreType.DMA((2, 2, pieces)),
        recv_sem=pltpu.SemaphoreType.DMA((2, 2, pieces)),
        mine_sem=pltpu.SemaphoreType.DMA((len(cuts),)),
    )

    def group(name, shapes):
        scratch.update({f"{name}{i}": shape for i, shape in enumerate(shapes)})
        return [f"{name}{i}" for i in range(len(shapes))]

    now_names = group("now", reduce_scratch(n, now, now_size, wide, side, lanes))
    if following is not None:
        args.update(following=following)
        specs.append(ANY)
        outs.update(
            following_slab=jax.ShapeDtypeStruct(slab.shape, slab.dtype),
            rest_out=jax.ShapeDtypeStruct((n * late, wide, side), f32),
        )
        early_names = group("early", gather_sems(n, half, gather_size))
        after_names = group("after", gather_sems(n, late, late_size))
        scratch.update(
            shelf=pltpu.VMEM((2, late_size, wide, side), f32),
            shelf_sem=pltpu.SemaphoreType.DMA((2,)),
        )
    if rest is not None:
        args.update(rest=rest)
        specs.append(ANY)
        outs.update(rest_piece=jax.ShapeDtypeStruct((late, wide, side), f32))
        late_names = group("late", reduce_scratch(n, late, late_size, wide, side, lanes))
        scratch.update(
            zs=pltpu.VMEM((n * late, wide, side), f32),
            zs_sem=pltpu.SemaphoreType.DMA(()),
        )
    names = list(args) + list(outs) + list(scratch)
    names[len(args) : len(args) + len(outs)] = [f"{name}_ref" for name in outs]
    names[: len(args)] = [f"{name}_ref" for name in args]

    def body(*refs):
        g = dict(zip(names, refs, strict=True))
        cols_ref, weights_ref, prev_ref, last_ref = (
            g[k] for k in ("cols_ref", "weights_ref", "prev_ref", "last_ref")
        )
        held, ring, part_ref, sums = g["held"], g["ring"], g["part"], g["sums"]
        in_code, in_step, out_code, out_step = (
            g[k] for k in ("in_code", "in_step", "out_code", "out_step")
        )
        me = lax.axis_index("blk")
        eye = diagonal(wide, lanes)

        def load(c):
            slot = c % slots
            return pltpu.make_async_copy(
                g["values_ref"].at[pl.ds(c * batch, batch)], ring.at[slot], g["ring_sem"].at[slot]
            )

        def shard(d, src):
            return pltpu.make_async_copy(
                src, held.at[pl.ds(d * blocks, blocks)], g["held_sem"].at[d]
            )

        load(0).start()
        for d in range(n):

            @pl.when(me == d)
            def _(d=d):
                shard(d, g["own_ref"]).start()

            @pl.when(me != d)
            def _(d=d):
                shard(d, g["slab_ref"].at[pl.ds(d * blocks, blocks)]).start()

        if rest is not None:
            zs_copy = pltpu.make_async_copy(g["rest_ref"], g["zs"], g["zs_sem"])
            zs_copy.start()
        greet(me, n)
        sums[items] = jnp.zeros((wide, side), f32)

        @pl.when(me == 0)
        def _():
            in_step[0] = jnp.zeros((rows, 1, lanes), f32)

        @pl.when(me == n - 1)
        def _():
            in_step[1] = jnp.zeros((rows, 1, lanes), f32)

        extra = []
        ends = []
        if following is not None:
            step, steps, finish = gather_steps(
                me, n, 0, half, gather_size, g["following_ref"], g["following_slab_ref"],
                *(g[k] for k in early_names),
            )
            extra.append((step, steps))
            ends.append(finish)
        if rest is not None:
            zs = g["zs"]

            def read_rest(d, c):
                return zs[pl.ds(d * late + c * late_size, late_size)]

            step, steps, finish = reduce_steps(
                me, n, late, late_size, eye, read_rest, zs, me * late,
                [g[k] for k in late_names], following is not None,
            )
            extra.append((step, steps))
            ends.append(finish)
            zs_copy.wait()

        for d in range(n):
            shard(d, g["own_ref"]).wait()

        def copies(way, c):
            to = {"blk": me + 1 - 2 * way}
            at = pl.ds(c * batch, batch)
            return [
                pltpu.make_async_remote_copy(
                    src_ref=src.at[way, at],
                    dst_ref=dst.at[way, at],
                    send_sem=g["send_sem"].at[way, kind, c],
                    recv_sem=g["recv_sem"].at[way, kind, c],
                    device_id=to,
                    device_id_type=MESH,
                )
                for kind, (src, dst) in enumerate(((out_code, in_code), (out_step, in_step)))
            ]

        def incoming(way, c):
            at = pl.ds(c * batch, batch)
            return decode(in_code[way, at], in_step[way, at], eye)

        def relay(way, c, has, goes):
            @pl.when((c >= 0) & (c < pieces) & has)
            def _():
                for one in copies(way, c):
                    one.wait_recv()

            @pl.when((c >= 0) & (c < pieces) & goes)
            def _():
                at = pl.ds(c * batch, batch)
                code, step = encode(part_ref[at] + incoming(way, c), eye)
                out_code[way, at] = code
                out_step[way, at] = step
                for one in copies(way, c):
                    one.start()

        first_steps = max([pieces + lag] + [steps for _, steps in extra])

        @pl.loop(0, first_steps)
        def _(s):
            @pl.when(s + 1 < pieces)
            def _():
                load(s + 1).start()

            @pl.when(s < pieces)
            def _():
                load(s).wait()
                for r in range(batch):
                    total = None
                    for k in range(per):
                        at = (s * batch + r) * per + k
                        term = weights_ref[at] * lax.dot_general(
                            held[cols_ref[at]],
                            ring[s % slots, r, k],
                            (((1,), (1,)), ((), ())),
                            preferred_element_type=f32,
                        )
                        total = term if total is None else total + term
                    part_ref[s * batch + r] = total

            relay(0, s - HOP * me, me > 0, me < n - 1)
            relay(1, s - HOP * (n - 1 - me), me < n - 1, me > 0)
            for step, steps in extra:

                @pl.when(s < steps)
                def _(step=step):
                    step(s)

            c = s - lag

            @pl.when((c >= 0) & (c < pieces))
            def _():
                total = part_ref[pl.ds(c * batch, batch)] + incoming(0, c) + incoming(1, c)
                high = total.astype(jnp.bfloat16)
                low = (total - high.astype(f32)).astype(jnp.bfloat16)
                for r in range(batch):
                    both = jnp.concatenate([high[r], low[r]], axis=0)
                    for k in range(per):
                        at = (c * batch + r) * per + k
                        pair = lax.dot_general(
                            both,
                            ring[c % slots, r, k],
                            (((1,), (0,)), ((), ())),
                            preferred_element_type=f32,
                        )
                        term = weights_ref[at] * (pair[:wide] + pair[wide:])
                        sums[at] = term + sums[prev_ref[at]]

        if rest is not None:
            rest_copy = pltpu.make_async_copy(
                g["zs"].at[pl.ds(me * late, late)], g["rest_piece_ref"], g["zs_sem"]
            )
            rest_copy.start()

        mine = g["mine"]

        @pl.loop(0, now)
        def _(i):
            mine[i] = sums[last_ref[me * blocks + i]]

        def read_now(d, c):
            first = d * blocks + c * now_size
            return jnp.stack([sums[last_ref[first + i]] for i in range(now_size)])

        step, steps, finish = reduce_steps(
            me, n, now, now_size, eye, read_now, mine, 0, [g[k] for k in now_names],
            following is not None,
        )
        second = [(step, steps)]
        ends.append(finish)
        if following is not None:
            step, steps, finish = gather_steps(
                me, n, half, late, late_size, g["following_ref"], g["following_slab_ref"],
                *(g[k] for k in after_names),
            )
            second.append((step, steps))
            ends.append(finish)
            shelf = g["shelf"]
            shelves = n * late // late_size
            per_shard = late // late_size

            def store(i):
                return pltpu.make_async_copy(
                    shelf.at[i % 2],
                    g["rest_out_ref"].at[pl.ds(i * late_size, late_size)],
                    g["shelf_sem"].at[i % 2],
                )

            def keep(i):
                @pl.when(i >= 2)
                def _():
                    store(i - 2).wait()

                first = i // per_shard * blocks + half + i % per_shard * late_size
                for j in range(late_size):
                    shelf[i % 2, j] = sums[last_ref[first + j]]
                store(i).start()

            second.append((keep, shelves))

        @pl.loop(0, max(steps for _, steps in second))
        def _(s):
            for step, steps in second:

                @pl.when(s < steps)
                def _(step=step):
                    step(s)

        mine_copies = [
            pltpu.make_async_copy(
                mine.at[pl.ds(a, b - a)], g[f"piece{i}_ref"], g["mine_sem"].at[i]
            )
            for i, (a, b) in enumerate(cuts)
        ]
        for one in mine_copies:
            one.start()

        @pl.loop(0, pieces)
        def _(c):
            @pl.when(me < n - 1)
            def _():
                for one in copies(0, c):
                    one.wait_send()

            @pl.when(me > 0)
            def _():
                for one in copies(1, c):
                    one.wait_send()

        for finish in ends:
            finish()
        if following is not None:
            for i in range(max(shelves - 2, 0), shelves):
                store(i).wait()
        if rest is not None:
            rest_copy.wait()
        for one in mine_copies:
            one.wait()

    results = pl.pallas_call(
        body,
        out_shape=list(outs.values()),
        in_specs=specs,
        out_specs=[ANY] * len(outs),
        scratch_shapes=list(scratch.values()),
        compiler_params=pltpu.CompilerParams(
            collective_id=2 + part, has_side_effects=True, vmem_limit_bytes=63 << 20
        ),
        name=f"stage_{part}",
    )(*args.values())
    return dict(zip(outs, results))


def all_sum(x, axis):
    n = lax.axis_size(axis)
    if n & (n - 1):
        return lax.psum(x, axis)
    bit = 1
    while bit < n:
        x = x + lax.ppermute(x, axis, [(i, i ^ bit) for i in range(n)])
        bit *= 2
    return x


def join(z_refs, early, b):
    here = [z_refs[2 * p + (0 if early else 1)][b] for p in range(len(z_refs) // 2)]
    return jnp.concatenate(here, axis=0)


def block_specs(pieces, batch, early_steps):
    specs = []
    for i, piece in enumerate(pieces):
        shape = (batch,) + piece.shape[1:]
        if i % 2 == 0:
            specs.append(pl.BlockSpec(shape, lambda i: (jnp.minimum(i, early_steps - 1), 0, 0)))
        else:
            specs.append(pl.BlockSpec(shape, lambda i: (jnp.maximum(i - early_steps, 0), 0, 0)))
    return specs


def halves(x):
    high = x.astype(jnp.bfloat16)
    return high, (x - high.astype(jnp.float32)).astype(jnp.bfloat16)


def outer(x, y):
    return lax.dot_general(x, y, (((1,), (1,)), ((), ())), preferred_element_type=jnp.float32)


def gram_of(pieces):
    early, late = pieces[0].shape[0], pieces[1].shape[0]
    side = pieces[0].shape[2]
    width = sum(piece.shape[1] for piece in pieces[::2])
    batch = divisor(math.gcd(early, late), 8)

    def body(*refs):
        *z_refs, out_ref, main, cross = refs

        @pl.when(pl.program_id(0) == 0)
        def _():
            main[...] = jnp.zeros_like(main)
            cross[...] = jnp.zeros_like(cross)

        for first in (True, False):

            @pl.when((pl.program_id(0) < early // batch) == first)
            def _(first=first):
                for b in range(batch):
                    high, low = halves(join(z_refs, first, b))
                    main[...] += outer(high, high)
                    cross[...] += outer(high, low)

        @pl.when(pl.program_id(0) == pl.num_programs(0) - 1)
        def _():
            out_ref[...] = main[...] + (cross[...] + cross[...].T)

    return pl.pallas_call(
        body,
        out_shape=jax.ShapeDtypeStruct((width, width), jnp.float32),
        grid=((early + late) // batch,),
        in_specs=block_specs(pieces, batch, early // batch),
        out_specs=pl.BlockSpec((width, width), lambda i: (0, 0)),
        scratch_shapes=[pltpu.VMEM((width, width), jnp.float32)] * 2,
        name="gram",
    )(*pieces)


def crossed(x, y):
    return lax.dot_general(x, y, (((0,), (1,)), ((), ())), preferred_element_type=jnp.float32)


def solve(pieces, inverse):
    early, late = pieces[0].shape[0], pieces[1].shape[0]
    side = pieces[0].shape[2]
    width = sum(piece.shape[1] for piece in pieces[::2])
    batch = divisor(math.gcd(early, late), 8)

    def body(*refs):
        *z_refs, inverse_ref, out_ref = refs
        inv_high, inv_low = halves(inverse_ref[...])
        inv_twice = jnp.concatenate([inv_high, inv_high], axis=1)
        for first in (True, False):

            @pl.when((pl.program_id(0) < early // batch) == first)
            def _(first=first):
                for b in range(batch):
                    high, low = halves(join(z_refs, first, b))
                    both = jnp.concatenate([high, low], axis=0)
                    out_ref[b] = crossed(both, inv_twice) + crossed(high, inv_low)

    return pl.pallas_call(
        body,
        out_shape=jax.ShapeDtypeStruct((early + late, side, width), jnp.float32),
        grid=((early + late) // batch,),
        in_specs=block_specs(pieces, batch, early // batch)
        + [pl.BlockSpec((width, width), lambda i: (0, 0))],
        out_specs=pl.BlockSpec((batch, side, width), lambda i: (i, 0, 0)),
        name="solve",
    )(*pieces, inverse)


def local(values, scales, pattern, omega):
    rows, per = pattern.shape
    blocks, side, width = omega.shape
    n = lax.axis_size("blk")
    items = rows * per
    columns = blocks * n
    cols = pattern.reshape(-1) - lax.axis_index("row") * columns
    weights = scales.astype(jnp.float32).reshape(-1)
    slot = jnp.arange(items)
    same = cols[:, None] == cols[None, :]
    prev = jnp.max(jnp.where(same & (slot[None, :] < slot[:, None]), slot[None, :], -1), axis=1)
    prev = jnp.where(prev < 0, items, prev)
    hits = jnp.arange(columns)[:, None] == cols[None, :]
    last = jnp.max(jnp.where(hits, slot[None, :], -1), axis=1)
    last = jnp.where(last < 0, items, last)

    parts = 4
    wide = width // parts
    turned = jnp.transpose(omega, (0, 2, 1)).reshape(blocks, parts, wide, side)
    own = [turned[:, p] for p in range(parts)]
    slab = gather(own[0], n)
    rest = None
    pieces = []
    for p in range(parts):
        following = own[p + 1] if p + 1 < parts else None
        done = stage(p, values, own[p], slab, (cols, weights, prev, last), n, following, rest)
        if p:
            pieces.append(done["rest_piece"])
        if p + 1 < parts:
            pieces.append(done["piece0"])
            slab, rest = done["following_slab"], done["rest_out"]
        else:
            pieces += [done["piece0"], done["piece1"]]

    total_rows = columns * side * lax.axis_size("row")
    gram = all_sum(all_sum(gram_of(pieces), "row"), "blk") / total_rows
    lower = jnp.linalg.cholesky(gram)
    inverse = jax.scipy.linalg.solve_triangular(lower, jnp.eye(width, dtype=jnp.float32), lower=True)
    return solve(pieces, inverse), lower.T


def solution(mesh):
    return jax.shard_map(
        local,
        mesh=mesh,
        in_specs=(
            P("row", "blk", None, None),
            P("row", "blk"),
            P("row", "blk"),
            P(("row", "blk"), None, None),
        ),
        out_specs=(P(("row", "blk"), None, None), P()),
        check_vma=False,
    )
```

```python
import math

import jax
import jax.numpy as jnp
from jax import lax
from jax.experimental import pallas as pl
from jax.experimental.pallas import tpu as pltpu
from jax.sharding import PartitionSpec as P

MESH = pl.DeviceIdType.MESH
LEVELS = 32767.0
TINY = 1e-30
HOP = 2
ANY = pl.BlockSpec(memory_space=pl.ANY)
SMEM = pl.BlockSpec(memory_space=pltpu.SMEM)


def divisor(n, most):
    return max(d for d in range(1, most + 1) if n % d == 0)


def diagonal(height, width):
    shape = (height, width)
    return lax.broadcasted_iota(jnp.int32, shape, 0) == lax.broadcasted_iota(jnp.int32, shape, 1)


def encode(x, eye):
    peak = jnp.max(jnp.max(jnp.abs(x), axis=0, keepdims=True), axis=2, keepdims=True)
    live = peak > TINY
    inverse = jnp.where(live, LEVELS / jnp.where(live, peak, 1.0), 0.0)
    code = jnp.round(x * inverse).astype(jnp.int32).astype(jnp.int16)
    step = jnp.sum(jnp.where(eye[None], peak * (1.0 / LEVELS), 0.0), axis=1, keepdims=True)
    return code, step


def decode(code, step, eye):
    column = jnp.sum(jnp.where(eye[None], step, 0.0), axis=2, keepdims=True)
    return code.astype(jnp.int32).astype(jnp.float32) * column


def greet(me, n):
    barrier = pltpu.get_barrier_semaphore()

    @pl.when(me > 0)
    def _():
        pl.semaphore_signal(barrier, inc=1, device_id={"blk": me - 1}, device_id_type=MESH)

    @pl.when(me < n - 1)
    def _():
        pl.semaphore_signal(barrier, inc=1, device_id={"blk": me + 1}, device_id_type=MESH)

    peers = jnp.where(me > 0, 1, 0) + jnp.where(me < n - 1, 1, 0)
    pl.semaphore_wait(barrier, peers)


def gather_steps(me, n, base, count, size, own_ref, slab_ref, send_sem, recv_sem):
    blocks = own_ref.shape[0]
    pieces = count // size

    def copy(way, t, c, owner):
        here = slab_ref.at[pl.ds(owner * blocks + base + c * size, size)]
        return pltpu.make_async_remote_copy(
            src_ref=here,
            dst_ref=here,
            send_sem=send_sem.at[way, t, c],
            recv_sem=recv_sem.at[way, t, c],
            device_id={"blk": me + 1 - 2 * way},
            device_id_type=MESH,
        )

    def first(way, c):
        return pltpu.make_async_remote_copy(
            src_ref=own_ref.at[pl.ds(base + c * size, size)],
            dst_ref=slab_ref.at[pl.ds(me * blocks + base + c * size, size)],
            send_sem=send_sem.at[way, 0, c],
            recv_sem=recv_sem.at[way, 0, c],
            device_id={"blk": me + 1 - 2 * way},
            device_id_type=MESH,
        )

    def has(way, t):
        behind = me if way == 0 else n - 1 - me
        return behind >= t

    def goes(way):
        return me < n - 1 if way == 0 else me > 0

    def owner_of(way, t):
        return me - t if way == 0 else me + t

    def step(v):
        t = v // pieces
        c = v % pieces
        for way in (0, 1):

            @pl.when((t == 0) & goes(way))
            def _(way=way):
                first(way, c).start()

            @pl.when((t > 0) & has(way, t))
            def _(way=way):
                copy(way, t - 1, c, owner_of(way, t)).wait_recv()

            @pl.when((t > 0) & (t < n - 1) & has(way, t) & goes(way))
            def _(way=way):
                copy(way, t, c, owner_of(way, t)).start()

    def finish():
        @pl.loop(0, (n - 1) * pieces)
        def _(v):
            t = v // pieces
            c = v % pieces
            for way in (0, 1):

                @pl.when(has(way, t) & goes(way))
                def _(way=way):
                    copy(way, t, c, me).wait_send()

    return step, n * pieces, finish


def gather_sems(n, count, size):
    return [pltpu.SemaphoreType.DMA((2, n - 1, count // size))] * 2


def gather(omega, n, parts):
    blocks, side, width = omega.shape
    wide = width // parts
    size = divisor(blocks, 4)
    pieces = blocks // size

    def body(omega_ref, *refs):
        slab_ref, *own_refs = refs[: 1 + parts]
        raw, turned, raw_sem, own_sem, *sems = refs[1 + parts :]
        me = lax.axis_index("blk")

        def load(c):
            at = pl.ds(c * size, size)
            return pltpu.make_async_copy(omega_ref.at[at], raw.at[at], raw_sem.at[c])

        def keep(p, c):
            at = pl.ds(c * size, size)
            return pltpu.make_async_copy(turned.at[p, at], own_refs[p].at[at], own_sem.at[p, c])

        for c in range(pieces):
            load(c).start()
        greet(me, n)
        step, steps, finish = gather_steps(me, n, 0, blocks, size, turned.at[0], slab_ref, *sems)

        @pl.loop(0, steps)
        def _(s):
            @pl.when(s < pieces)
            def _():
                load(s).wait()
                for i in range(size):
                    block = raw[s * size + i].T
                    for p in range(parts):
                        turned[p, s * size + i] = block[p * wide : (p + 1) * wide]

            step(s)

            @pl.when(s < pieces)
            def _():
                for p in range(parts):
                    keep(p, s).start()

        finish()

        @pl.loop(0, pieces)
        def _(c):
            for p in range(parts):
                keep(p, c).wait()

    return pl.pallas_call(
        body,
        out_shape=[jax.ShapeDtypeStruct((n * blocks, wide, side), omega.dtype)]
        + [jax.ShapeDtypeStruct((blocks, wide, side), omega.dtype)] * parts,
        in_specs=[ANY],
        out_specs=[ANY] * (1 + parts),
        scratch_shapes=[
            pltpu.VMEM(omega.shape, omega.dtype),
            pltpu.VMEM((parts, blocks, wide, side), omega.dtype),
            pltpu.SemaphoreType.DMA((pieces,)),
            pltpu.SemaphoreType.DMA((parts, pieces)),
        ]
        + gather_sems(n, blocks, size),
        compiler_params=pltpu.CompilerParams(collective_id=1, has_side_effects=True),
        name="gather",
    )(omega)


def reduce_scratch(n, count, size, wide, side, lanes):
    far = (n - 1) * count
    sems = pltpu.SemaphoreType.DMA((2, 2, far // size))
    code = pltpu.VMEM((2, far, wide, side), jnp.int16)
    step = pltpu.VMEM((2, far // size, 1, lanes), jnp.float32)
    return [code, step, code, step, sems, sems]


def reduce_steps(me, n, count, size, eye, read, total, base, scratch, beside, start):
    in_code, in_step, out_code, out_step, send_sem, recv_sem = scratch
    pieces = count // size
    reach = (n - 1) * pieces
    far = ((n - 1 - me) * pieces, me * pieces)
    hop = max(pieces, HOP) if beside else HOP

    def copies(way, u):
        to = {"blk": me + 1 - 2 * way}
        pairs = (out_code, in_code, pl.ds(u * size, size)), (out_step, in_step, pl.ds(u, 1))
        return [
            pltpu.make_async_remote_copy(
                src_ref=src.at[way, here],
                dst_ref=dst.at[way, here],
                send_sem=send_sem.at[way, kind, u],
                recv_sem=recv_sem.at[way, kind, u],
                device_id=to,
                device_id_type=MESH,
            )
            for kind, (src, dst, here) in enumerate(pairs)
        ]

    def incoming(way, u):
        return decode(in_code[way, pl.ds(u * size, size)], in_step[way, pl.ds(u, 1)], eye)

    def push(way, u, value):
        code, step = encode(value, eye)
        out_code[way, pl.ds(u * size, size)] = code
        out_step[way, pl.ds(u, 1)] = step
        for one in copies(way, u):
            one.start()

    def source(way, u):
        d = n - 1 - u // pieces if way == 0 else u // pieces
        return read(d, u % pieces)

    def step(s):
        for way in (0, 1):
            behind = me if way == 0 else n - 1 - me
            u = s - start - hop * behind
            inside = (u >= 0) & (u < far[way])

            @pl.when(inside & (behind == 0))
            def _(way=way, u=u):
                push(way, u, source(way, u))

            @pl.when(inside & (behind > 0))
            def _(way=way, u=u):
                for one in copies(way, u):
                    one.wait_recv()
                push(way, u, source(way, u) + incoming(way, u))

            @pl.when((behind > 0) & (u >= far[way]) & (u < far[way] + pieces))
            def _(way=way, u=u):
                for one in copies(way, u):
                    one.wait_recv()
                at = pl.ds(base + (u - far[way]) * size, size)
                total[at] = total[at] + incoming(way, u)

    def finish():
        @pl.loop(0, reach)
        def _(u):
            for way in (0, 1):

                @pl.when(u < far[way])
                def _(way=way):
                    for one in copies(way, u):
                        one.wait_send()

    return step, start + max([reach] + [hop * b + (n - b) * pieces for b in range(1, n)]), finish


def stage(part, values, own, slab, tables, n, following=None, rest=None):
    rows, per, side, _ = values.shape
    blocks, wide, _ = own.shape
    lanes = 128
    items = rows * per
    columns = n * blocks
    batch = divisor(rows, 4)
    pieces = rows // batch
    lag = HOP * (n - 1)
    slots = lag + 2
    half = blocks // 2
    late = blocks - half
    now = half if following is not None else blocks
    now_size = divisor(now, 4 if following is not None else 8)
    late_size = divisor(late, 4)
    gather_size = divisor(half, 4)
    f32 = jnp.float32

    args = dict(zip(("cols", "weights", "prev", "last"), tables))
    args.update(values=values, own=own, slab=slab)
    specs = [SMEM] * 4 + [ANY] * 3
    cuts = [(0, half)] + ([(half, blocks)] if following is None else [])
    outs = {
        f"piece{i}": jax.ShapeDtypeStruct((b - a, wide, side), f32) for i, (a, b) in enumerate(cuts)
    }
    scratch = dict(
        held=pltpu.VMEM((columns, wide, side), own.dtype),
        ring=pltpu.VMEM((slots, batch, per, side, side), values.dtype),
        part=pltpu.VMEM((rows, wide, side), f32),
        in_code=pltpu.VMEM((2, rows, wide, side), jnp.int16),
        in_step=pltpu.VMEM((2, pieces, 1, lanes), f32),
        out_code=pltpu.VMEM((2, rows, wide, side), jnp.int16),
        out_step=pltpu.VMEM((2, pieces, 1, lanes), f32),
        sums=pltpu.VMEM((items + 1, wide, side), f32),
        mine=pltpu.VMEM((now, wide, side), f32),
        held_sem=pltpu.SemaphoreType.DMA((n,)),
        ring_sem=pltpu.SemaphoreType.DMA((slots,)),
        send_sem=pltpu.SemaphoreType.DMA((2, 2, pieces)),
        recv_sem=pltpu.SemaphoreType.DMA((2, 2, pieces)),
        mine_sem=pltpu.SemaphoreType.DMA((len(cuts),)),
    )

    def group(name, shapes):
        scratch.update({f"{name}{i}": shape for i, shape in enumerate(shapes)})
        return [f"{name}{i}" for i in range(len(shapes))]

    now_names = group("now", reduce_scratch(n, now, now_size, wide, side, lanes))
    if following is not None:
        args.update(following=following)
        specs.append(ANY)
        outs.update(
            following_slab=jax.ShapeDtypeStruct(slab.shape, slab.dtype),
            rest_out=jax.ShapeDtypeStruct((n * late, wide, side), f32),
        )
        early_names = group("early", gather_sems(n, half, gather_size))
        after_names = group("after", gather_sems(n, late, late_size))
        scratch.update(
            shelf=pltpu.VMEM((2, late_size, wide, side), f32),
            shelf_sem=pltpu.SemaphoreType.DMA((2,)),
        )
    if rest is not None:
        args.update(rest=rest)
        specs.append(ANY)
        outs.update(rest_piece=jax.ShapeDtypeStruct((late, wide, side), f32))
        late_names = group("late", reduce_scratch(n, late, late_size, wide, side, lanes))
        scratch.update(
            zs=pltpu.VMEM((n * late, wide, side), f32),
            zs_sem=pltpu.SemaphoreType.DMA(()),
        )
    names = list(args) + list(outs) + list(scratch)
    names[len(args) : len(args) + len(outs)] = [f"{name}_ref" for name in outs]
    names[: len(args)] = [f"{name}_ref" for name in args]

    def body(*refs):
        g = dict(zip(names, refs, strict=True))
        cols_ref, weights_ref, prev_ref, last_ref = (
            g[k] for k in ("cols_ref", "weights_ref", "prev_ref", "last_ref")
        )
        held, ring, part_ref, sums = g["held"], g["ring"], g["part"], g["sums"]
        in_code, in_step, out_code, out_step = (
            g[k] for k in ("in_code", "in_step", "out_code", "out_step")
        )
        me = lax.axis_index("blk")
        eye = diagonal(wide, lanes)

        def load(c):
            slot = c % slots
            return pltpu.make_async_copy(
                g["values_ref"].at[pl.ds(c * batch, batch)], ring.at[slot], g["ring_sem"].at[slot]
            )

        def shard(d, src):
            return pltpu.make_async_copy(
                src, held.at[pl.ds(d * blocks, blocks)], g["held_sem"].at[d]
            )

        load(0).start()
        for d in range(n):

            @pl.when(me == d)
            def _(d=d):
                shard(d, g["own_ref"]).start()

            @pl.when(me != d)
            def _(d=d):
                shard(d, g["slab_ref"].at[pl.ds(d * blocks, blocks)]).start()

        if rest is not None:
            zs_copy = pltpu.make_async_copy(g["rest_ref"], g["zs"], g["zs_sem"])
            zs_copy.start()
        greet(me, n)
        sums[items] = jnp.zeros((wide, side), f32)

        @pl.when(me == 0)
        def _():
            in_step[0] = jnp.zeros((pieces, 1, lanes), f32)

        @pl.when(me == n - 1)
        def _():
            in_step[1] = jnp.zeros((pieces, 1, lanes), f32)

        extra = []
        ends = []
        if following is not None:
            step, steps, finish = gather_steps(
                me, n, 0, half, gather_size, g["following_ref"], g["following_slab_ref"],
                *(g[k] for k in early_names),
            )
            lead = min(2, steps)
            extra.append((lambda s, step=step: step(s + lead), steps - lead))
            ends.append(finish)
            for v in range(lead):
                step(v)
        if rest is not None:
            zs = g["zs"]

            def read_rest(d, c):
                return zs[pl.ds(d * late + c * late_size, late_size)]

            step, steps, finish = reduce_steps(
                me, n, late, late_size, eye, read_rest, zs, me * late,
                [g[k] for k in late_names], following is not None,
                max(half // gather_size - 2, 0) if following is not None else 0,
            )
            extra.append((step, steps))
            ends.append(finish)
            zs_copy.wait()

        for d in range(n):
            shard(d, g["own_ref"]).wait()

        def copies(way, c):
            to = {"blk": me + 1 - 2 * way}
            pairs = (
                (out_code, in_code, pl.ds(c * batch, batch)),
                (out_step, in_step, pl.ds(c, 1)),
            )
            return [
                pltpu.make_async_remote_copy(
                    src_ref=src.at[way, here],
                    dst_ref=dst.at[way, here],
                    send_sem=g["send_sem"].at[way, kind, c],
                    recv_sem=g["recv_sem"].at[way, kind, c],
                    device_id=to,
                    device_id_type=MESH,
                )
                for kind, (src, dst, here) in enumerate(pairs)
            ]

        def incoming(way, c):
            code = in_code[way, pl.ds(c * batch, batch)]
            return decode(code, in_step[way, pl.ds(c, 1)], eye)

        def relay(way, c, has, goes):
            @pl.when((c >= 0) & (c < pieces) & has)
            def _():
                for one in copies(way, c):
                    one.wait_recv()

            @pl.when((c >= 0) & (c < pieces) & goes)
            def _():
                at = pl.ds(c * batch, batch)
                code, step = encode(part_ref[at] + incoming(way, c), eye)
                out_code[way, at] = code
                out_step[way, pl.ds(c, 1)] = step
                for one in copies(way, c):
                    one.start()

        first_steps = max([pieces + lag] + [steps for _, steps in extra])
        if following is not None:
            late_step, late_steps, finish = gather_steps(
                me, n, half, late, late_size, g["following_ref"], g["following_slab_ref"],
                *(g[k] for k in after_names),
            )
            ends.append(finish)
            ahead = late // late_size

        @pl.loop(0, first_steps)
        def _(s):
            @pl.when(s + 1 < pieces)
            def _():
                load(s + 1).start()

            @pl.when(s < pieces)
            def _():
                load(s).wait()
                for r in range(batch):
                    total = None
                    for k in range(per):
                        at = (s * batch + r) * per + k
                        term = weights_ref[at] * lax.dot_general(
                            held[cols_ref[at]],
                            ring[s % slots, r, k],
                            (((1,), (1,)), ((), ())),
                            preferred_element_type=f32,
                        )
                        total = term if total is None else total + term
                    part_ref[s * batch + r] = total

            relay(0, s - HOP * me, me > 0, me < n - 1)
            relay(1, s - HOP * (n - 1 - me), me < n - 1, me > 0)
            for step, steps in extra:

                @pl.when(s < steps)
                def _(step=step):
                    step(s)

            if following is not None:

                @pl.when(s >= first_steps - ahead)
                def _():
                    late_step(s - (first_steps - ahead))

            c = s - lag

            @pl.when((c >= 0) & (c < pieces))
            def _():
                total = part_ref[pl.ds(c * batch, batch)] + incoming(0, c) + incoming(1, c)
                high = total.astype(jnp.bfloat16)
                low = (total - high.astype(f32)).astype(jnp.bfloat16)
                for r in range(batch):
                    both = jnp.concatenate([high[r], low[r]], axis=0)
                    for k in range(per):
                        at = (c * batch + r) * per + k
                        pair = lax.dot_general(
                            both,
                            ring[c % slots, r, k],
                            (((1,), (0,)), ((), ())),
                            preferred_element_type=f32,
                        )
                        term = weights_ref[at] * (pair[:wide] + pair[wide:])
                        sums[at] = term + sums[prev_ref[at]]

        if rest is not None:
            rest_copy = pltpu.make_async_copy(
                g["zs"].at[pl.ds(me * late, late)], g["rest_piece_ref"], g["zs_sem"]
            )
            rest_copy.start()

        mine = g["mine"]

        @pl.loop(0, now)
        def _(i):
            mine[i] = sums[last_ref[me * blocks + i]]

        def read_now(d, c):
            first = d * blocks + c * now_size
            return jnp.stack([sums[last_ref[first + i]] for i in range(now_size)])

        step, steps, finish = reduce_steps(
            me, n, now, now_size, eye, read_now, mine, 0, [g[k] for k in now_names],
            following is not None, 0,
        )
        second = [(step, steps)]
        ends.append(finish)
        if following is not None:
            second.append((lambda s: late_step(s + ahead), late_steps - ahead))
            shelf = g["shelf"]
            shelves = n * late // late_size
            per_shard = late // late_size

            def store(i):
                return pltpu.make_async_copy(
                    shelf.at[i % 2],
                    g["rest_out_ref"].at[pl.ds(i * late_size, late_size)],
                    g["shelf_sem"].at[i % 2],
                )

            def keep(i):
                @pl.when(i >= 2)
                def _():
                    store(i - 2).wait()

                first = i // per_shard * blocks + half + i % per_shard * late_size
                for j in range(late_size):
                    shelf[i % 2, j] = sums[last_ref[first + j]]
                store(i).start()

            second.append((keep, shelves))

        @pl.loop(0, max(steps for _, steps in second))
        def _(s):
            for step, steps in second:

                @pl.when(s < steps)
                def _(step=step):
                    step(s)

        mine_copies = [
            pltpu.make_async_copy(
                mine.at[pl.ds(a, b - a)], g[f"piece{i}_ref"], g["mine_sem"].at[i]
            )
            for i, (a, b) in enumerate(cuts)
        ]
        for one in mine_copies:
            one.start()

        @pl.loop(0, pieces)
        def _(c):
            @pl.when(me < n - 1)
            def _():
                for one in copies(0, c):
                    one.wait_send()

            @pl.when(me > 0)
            def _():
                for one in copies(1, c):
                    one.wait_send()

        for finish in ends:
            finish()
        if following is not None:
            for i in range(max(shelves - 2, 0), shelves):
                store(i).wait()
        if rest is not None:
            rest_copy.wait()
        for one in mine_copies:
            one.wait()

    results = pl.pallas_call(
        body,
        out_shape=list(outs.values()),
        in_specs=specs,
        out_specs=[ANY] * len(outs),
        scratch_shapes=list(scratch.values()),
        compiler_params=pltpu.CompilerParams(
            collective_id=2 + part, has_side_effects=True, vmem_limit_bytes=63 << 20
        ),
        name=f"stage_{part}",
    )(*args.values())
    return dict(zip(outs, results))


def all_sum(x, axis):
    n = lax.axis_size(axis)
    if n & (n - 1):
        return lax.psum(x, axis)
    bit = 1
    while bit < n:
        x = x + lax.ppermute(x, axis, [(i, i ^ bit) for i in range(n)])
        bit *= 2
    return x


def join(z_refs, early, b):
    here = [z_refs[2 * p + (0 if early else 1)][b] for p in range(len(z_refs) // 2)]
    return jnp.concatenate(here, axis=0)


def block_specs(pieces, batch, early_steps):
    specs = []
    for i, piece in enumerate(pieces):
        shape = (batch,) + piece.shape[1:]
        if i % 2 == 0:
            specs.append(pl.BlockSpec(shape, lambda i: (jnp.minimum(i, early_steps - 1), 0, 0)))
        else:
            specs.append(pl.BlockSpec(shape, lambda i: (jnp.maximum(i - early_steps, 0), 0, 0)))
    return specs


def halves(x):
    high = x.astype(jnp.bfloat16)
    return high, (x - high.astype(jnp.float32)).astype(jnp.bfloat16)


def outer(x, y):
    return lax.dot_general(x, y, (((1,), (1,)), ((), ())), preferred_element_type=jnp.float32)


def gram_of(pieces):
    early, late = pieces[0].shape[0], pieces[1].shape[0]
    side = pieces[0].shape[2]
    width = sum(piece.shape[1] for piece in pieces[::2])
    batch = divisor(math.gcd(early, late), 8)

    def body(*refs):
        *z_refs, out_ref, main, cross = refs

        @pl.when(pl.program_id(0) == 0)
        def _():
            main[...] = jnp.zeros_like(main)
            cross[...] = jnp.zeros_like(cross)

        for first in (True, False):

            @pl.when((pl.program_id(0) < early // batch) == first)
            def _(first=first):
                for b in range(batch):
                    high, low = halves(join(z_refs, first, b))
                    main[...] += outer(high, high)
                    cross[...] += outer(high, low)

        @pl.when(pl.program_id(0) == pl.num_programs(0) - 1)
        def _():
            out_ref[...] = main[...] + (cross[...] + cross[...].T)

    return pl.pallas_call(
        body,
        out_shape=jax.ShapeDtypeStruct((width, width), jnp.float32),
        grid=((early + late) // batch,),
        in_specs=block_specs(pieces, batch, early // batch),
        out_specs=pl.BlockSpec((width, width), lambda i: (0, 0)),
        scratch_shapes=[pltpu.VMEM((width, width), jnp.float32)] * 2,
        name="gram",
    )(*pieces)


def crossed(x, y):
    return lax.dot_general(x, y, (((0,), (1,)), ((), ())), preferred_element_type=jnp.float32)


def solve(pieces, inverse):
    early, late = pieces[0].shape[0], pieces[1].shape[0]
    side = pieces[0].shape[2]
    width = sum(piece.shape[1] for piece in pieces[::2])
    batch = divisor(math.gcd(early, late), 8)

    def body(*refs):
        *z_refs, inverse_ref, out_ref = refs
        inv_high, inv_low = halves(inverse_ref[...])
        inv_twice = jnp.concatenate([inv_high, inv_high], axis=1)
        for first in (True, False):

            @pl.when((pl.program_id(0) < early // batch) == first)
            def _(first=first):
                for b in range(batch):
                    high, low = halves(join(z_refs, first, b))
                    both = jnp.concatenate([high, low], axis=0)
                    out_ref[b] = crossed(both, inv_twice) + crossed(high, inv_low)

    return pl.pallas_call(
        body,
        out_shape=jax.ShapeDtypeStruct((early + late, side, width), jnp.float32),
        grid=((early + late) // batch,),
        in_specs=block_specs(pieces, batch, early // batch)
        + [pl.BlockSpec((width, width), lambda i: (0, 0))],
        out_specs=pl.BlockSpec((batch, side, width), lambda i: (i, 0, 0)),
        name="solve",
    )(*pieces, inverse)


def local(values, scales, pattern, omega):
    rows, per = pattern.shape
    blocks, side, width = omega.shape
    n = lax.axis_size("blk")
    items = rows * per
    columns = blocks * n
    cols = pattern.reshape(-1) - lax.axis_index("row") * columns
    weights = scales.astype(jnp.float32).reshape(-1)
    slot = jnp.arange(items)
    same = cols[:, None] == cols[None, :]
    prev = jnp.max(jnp.where(same & (slot[None, :] < slot[:, None]), slot[None, :], -1), axis=1)
    prev = jnp.where(prev < 0, items, prev)
    hits = jnp.arange(columns)[:, None] == cols[None, :]
    last = jnp.max(jnp.where(hits, slot[None, :], -1), axis=1)
    last = jnp.where(last < 0, items, last)

    parts = 4
    slab, *own = gather(omega, n, parts)
    rest = None
    pieces = []
    for p in range(parts):
        following = own[p + 1] if p + 1 < parts else None
        done = stage(p, values, own[p], slab, (cols, weights, prev, last), n, following, rest)
        if p:
            pieces.append(done["rest_piece"])
        if p + 1 < parts:
            pieces.append(done["piece0"])
            slab, rest = done["following_slab"], done["rest_out"]
        else:
            pieces += [done["piece0"], done["piece1"]]

    total_rows = columns * side * lax.axis_size("row")
    gram = all_sum(all_sum(gram_of(pieces), "row"), "blk") / total_rows
    lower = jnp.linalg.cholesky(gram)
    inverse = jax.scipy.linalg.solve_triangular(lower, jnp.eye(width, dtype=jnp.float32), lower=True)
    return solve(pieces, inverse), lower.T


def solution(mesh):
    return jax.shard_map(
        local,
        mesh=mesh,
        in_specs=(
            P("row", "blk", None, None),
            P("row", "blk"),
            P("row", "blk"),
            P(("row", "blk"), None, None),
        ),
        out_specs=(P(("row", "blk"), None, None), P()),
        check_vma=False,
    )
```

```python
import math

import jax
import jax.numpy as jnp
from jax import lax
from jax.experimental import pallas as pl
from jax.experimental.pallas import tpu as pltpu
from jax.sharding import PartitionSpec as P

MESH = pl.DeviceIdType.MESH
LEVELS = 32767.0
TINY = 1e-30
HOP = 2
ANY = pl.BlockSpec(memory_space=pl.ANY)
SMEM = pl.BlockSpec(memory_space=pltpu.SMEM)


def divisor(n, most):
    return max(d for d in range(1, most + 1) if n % d == 0)


def diagonal(height, width):
    shape = (height, width)
    return lax.broadcasted_iota(jnp.int32, shape, 0) == lax.broadcasted_iota(jnp.int32, shape, 1)


def encode(x, eye):
    peak = jnp.max(jnp.max(jnp.abs(x), axis=0, keepdims=True), axis=2, keepdims=True)
    live = peak > TINY
    inverse = jnp.where(live, LEVELS / jnp.where(live, peak, 1.0), 0.0)
    code = jnp.round(x * inverse).astype(jnp.int32).astype(jnp.int16)
    step = jnp.sum(jnp.where(eye[None], peak * (1.0 / LEVELS), 0.0), axis=1, keepdims=True)
    return code, step


def decode(code, step, eye):
    column = jnp.sum(jnp.where(eye[None], step, 0.0), axis=2, keepdims=True)
    return code.astype(jnp.int32).astype(jnp.float32) * column


def greet(me, n):
    barrier = pltpu.get_barrier_semaphore()

    @pl.when(me > 0)
    def _():
        pl.semaphore_signal(barrier, inc=1, device_id={"blk": me - 1}, device_id_type=MESH)

    @pl.when(me < n - 1)
    def _():
        pl.semaphore_signal(barrier, inc=1, device_id={"blk": me + 1}, device_id_type=MESH)

    peers = jnp.where(me > 0, 1, 0) + jnp.where(me < n - 1, 1, 0)
    pl.semaphore_wait(barrier, peers)


def gather_steps(me, n, base, count, size, own_ref, slab_ref, send_sem, recv_sem):
    blocks = own_ref.shape[0]
    pieces = count // size

    def copy(way, t, c, owner):
        here = slab_ref.at[pl.ds(owner * blocks + base + c * size, size)]
        return pltpu.make_async_remote_copy(
            src_ref=here,
            dst_ref=here,
            send_sem=send_sem.at[way, t, c],
            recv_sem=recv_sem.at[way, t, c],
            device_id={"blk": me + 1 - 2 * way},
            device_id_type=MESH,
        )

    def first(way, c):
        return pltpu.make_async_remote_copy(
            src_ref=own_ref.at[pl.ds(base + c * size, size)],
            dst_ref=slab_ref.at[pl.ds(me * blocks + base + c * size, size)],
            send_sem=send_sem.at[way, 0, c],
            recv_sem=recv_sem.at[way, 0, c],
            device_id={"blk": me + 1 - 2 * way},
            device_id_type=MESH,
        )

    def has(way, t):
        behind = me if way == 0 else n - 1 - me
        return behind >= t

    def goes(way):
        return me < n - 1 if way == 0 else me > 0

    def owner_of(way, t):
        return me - t if way == 0 else me + t

    def step(v):
        t = v // pieces
        c = v % pieces
        for way in (0, 1):

            @pl.when((t == 0) & goes(way))
            def _(way=way):
                first(way, c).start()

            @pl.when((t > 0) & has(way, t))
            def _(way=way):
                copy(way, t - 1, c, owner_of(way, t)).wait_recv()

            @pl.when((t > 0) & (t < n - 1) & has(way, t) & goes(way))
            def _(way=way):
                copy(way, t, c, owner_of(way, t)).start()

    def finish():
        @pl.loop(0, (n - 1) * pieces)
        def _(v):
            t = v // pieces
            c = v % pieces
            for way in (0, 1):

                @pl.when(has(way, t) & goes(way))
                def _(way=way):
                    copy(way, t, c, me).wait_send()

    return step, n * pieces, finish


def gather_sems(n, count, size):
    return [pltpu.SemaphoreType.DMA((2, n - 1, count // size))] * 2


def gather(omega, n, parts):
    blocks, side, width = omega.shape
    wide = width // parts
    size = divisor(blocks, 4)
    pieces = blocks // size

    def body(omega_ref, *refs):
        slab_ref, *own_refs = refs[: 1 + parts]
        raw, turned, raw_sem, own_sem, *sems = refs[1 + parts :]
        me = lax.axis_index("blk")

        def load(c):
            at = pl.ds(c * size, size)
            return pltpu.make_async_copy(omega_ref.at[at], raw.at[at], raw_sem.at[c])

        def keep(p, c):
            at = pl.ds(c * size, size)
            return pltpu.make_async_copy(turned.at[p, at], own_refs[p].at[at], own_sem.at[p, c])

        for c in range(pieces):
            load(c).start()
        greet(me, n)
        step, steps, finish = gather_steps(me, n, 0, blocks, size, turned.at[0], slab_ref, *sems)

        @pl.loop(0, steps)
        def _(s):
            @pl.when(s < pieces)
            def _():
                load(s).wait()
                for i in range(size):
                    block = raw[s * size + i].T
                    for p in range(parts):
                        turned[p, s * size + i] = block[p * wide : (p + 1) * wide]

            step(s)

            @pl.when(s < pieces)
            def _():
                for p in range(parts):
                    keep(p, s).start()

        finish()

        @pl.loop(0, pieces)
        def _(c):
            for p in range(parts):
                keep(p, c).wait()

    return pl.pallas_call(
        body,
        out_shape=[jax.ShapeDtypeStruct((n * blocks, wide, side), omega.dtype)]
        + [jax.ShapeDtypeStruct((blocks, wide, side), omega.dtype)] * parts,
        in_specs=[ANY],
        out_specs=[ANY] * (1 + parts),
        scratch_shapes=[
            pltpu.VMEM(omega.shape, omega.dtype),
            pltpu.VMEM((parts, blocks, wide, side), omega.dtype),
            pltpu.SemaphoreType.DMA((pieces,)),
            pltpu.SemaphoreType.DMA((parts, pieces)),
        ]
        + gather_sems(n, blocks, size),
        compiler_params=pltpu.CompilerParams(collective_id=1, has_side_effects=True),
        name="gather",
    )(omega)


def reduce_scratch(n, count, size, wide, side, lanes):
    far = (n - 1) * count
    sems = pltpu.SemaphoreType.DMA((2, 2, far // size))
    code = pltpu.VMEM((2, far, wide, side), jnp.int16)
    step = pltpu.VMEM((2, far // size, 1, lanes), jnp.float32)
    return [code, step, code, step, sems, sems]


def reduce_steps(me, n, count, size, eye, read, total, base, scratch, beside, start):
    in_code, in_step, out_code, out_step, send_sem, recv_sem = scratch
    pieces = count // size
    reach = (n - 1) * pieces
    far = ((n - 1 - me) * pieces, me * pieces)
    hop = max(pieces, HOP) if beside else HOP

    def copies(way, u):
        to = {"blk": me + 1 - 2 * way}
        pairs = (out_code, in_code, pl.ds(u * size, size)), (out_step, in_step, pl.ds(u, 1))
        return [
            pltpu.make_async_remote_copy(
                src_ref=src.at[way, here],
                dst_ref=dst.at[way, here],
                send_sem=send_sem.at[way, kind, u],
                recv_sem=recv_sem.at[way, kind, u],
                device_id=to,
                device_id_type=MESH,
            )
            for kind, (src, dst, here) in enumerate(pairs)
        ]

    def incoming(way, u):
        return decode(in_code[way, pl.ds(u * size, size)], in_step[way, pl.ds(u, 1)], eye)

    def push(way, u, value):
        code, step = encode(value, eye)
        out_code[way, pl.ds(u * size, size)] = code
        out_step[way, pl.ds(u, 1)] = step
        for one in copies(way, u):
            one.start()

    def source(way, u):
        d = n - 1 - u // pieces if way == 0 else u // pieces
        return read(d, u % pieces)

    def step(s):
        for way in (0, 1):
            behind = me if way == 0 else n - 1 - me
            u = s - start - hop * behind
            inside = (u >= 0) & (u < far[way])

            @pl.when(inside & (behind == 0))
            def _(way=way, u=u):
                push(way, u, source(way, u))

            @pl.when(inside & (behind > 0))
            def _(way=way, u=u):
                for one in copies(way, u):
                    one.wait_recv()
                push(way, u, source(way, u) + incoming(way, u))

            @pl.when((behind > 0) & (u >= far[way]) & (u < far[way] + pieces))
            def _(way=way, u=u):
                for one in copies(way, u):
                    one.wait_recv()
                at = pl.ds(base + (u - far[way]) * size, size)
                total[at] = total[at] + incoming(way, u)

    def finish():
        @pl.loop(0, reach)
        def _(u):
            for way in (0, 1):

                @pl.when(u < far[way])
                def _(way=way):
                    for one in copies(way, u):
                        one.wait_send()

    return step, start + max([reach] + [hop * b + (n - b) * pieces for b in range(1, n)]), finish


def stage(part, values, own, slab, tables, n, following=None, rest=None):
    rows, per, side, _ = values.shape
    blocks, wide, _ = own.shape
    lanes = 128
    items = rows * per
    columns = n * blocks
    batch = divisor(rows, 4)
    pieces = rows // batch
    lag = HOP * (n - 1)
    slots = lag + 2
    half = blocks // 2
    late = blocks - half
    now = half if following is not None else blocks
    now_size = divisor(now, 4 if following is not None else 8)
    late_size = divisor(late, 4)
    gather_size = divisor(half, 4)
    f32 = jnp.float32

    args = dict(zip(("cols", "weights", "prev", "last"), tables))
    args.update(values=values, own=own, slab=slab)
    specs = [SMEM] * 4 + [ANY] * 3
    cuts = [(0, half)] + ([(half, blocks)] if following is None else [])
    outs = {
        f"piece{i}": jax.ShapeDtypeStruct((b - a, wide, side), f32) for i, (a, b) in enumerate(cuts)
    }
    scratch = dict(
        held=pltpu.VMEM((columns, wide, side), own.dtype),
        ring=pltpu.VMEM((slots, batch, per, side, side), values.dtype),
        part=pltpu.VMEM((rows, wide, side), f32),
        in_code=pltpu.VMEM((2, rows, wide, side), jnp.int16),
        in_step=pltpu.VMEM((2, pieces, 1, lanes), f32),
        out_code=pltpu.VMEM((2, rows, wide, side), jnp.int16),
        out_step=pltpu.VMEM((2, pieces, 1, lanes), f32),
        sums=pltpu.VMEM((items + 1, wide, side), f32),
        mine=pltpu.VMEM((now, wide, side), f32),
        held_sem=pltpu.SemaphoreType.DMA((n,)),
        ring_sem=pltpu.SemaphoreType.DMA((slots,)),
        send_sem=pltpu.SemaphoreType.DMA((2, 2, pieces)),
        recv_sem=pltpu.SemaphoreType.DMA((2, 2, pieces)),
        mine_sem=pltpu.SemaphoreType.DMA((len(cuts),)),
    )

    def group(name, shapes):
        scratch.update({f"{name}{i}": shape for i, shape in enumerate(shapes)})
        return [f"{name}{i}" for i in range(len(shapes))]

    now_names = group("now", reduce_scratch(n, now, now_size, wide, side, lanes))
    if following is not None:
        args.update(following=following)
        specs.append(ANY)
        outs.update(
            following_slab=jax.ShapeDtypeStruct(slab.shape, slab.dtype),
            rest_out=jax.ShapeDtypeStruct((n * late, wide, side), f32),
        )
        early_names = group("early", gather_sems(n, half, gather_size))
        after_names = group("after", gather_sems(n, late, late_size))
        scratch.update(
            shelf=pltpu.VMEM((2, late_size, wide, side), f32),
            shelf_sem=pltpu.SemaphoreType.DMA((2,)),
        )
    if rest is not None:
        args.update(rest=rest)
        specs.append(ANY)
        outs.update(rest_piece=jax.ShapeDtypeStruct((late, wide, side), f32))
        late_names = group("late", reduce_scratch(n, late, late_size, wide, side, lanes))
        scratch.update(
            zs=pltpu.VMEM((n * late, wide, side), f32),
            zs_sem=pltpu.SemaphoreType.DMA(()),
        )
    names = list(args) + list(outs) + list(scratch)
    names[len(args) : len(args) + len(outs)] = [f"{name}_ref" for name in outs]
    names[: len(args)] = [f"{name}_ref" for name in args]

    def body(*refs):
        g = dict(zip(names, refs, strict=True))
        cols_ref, weights_ref, prev_ref, last_ref = (
            g[k] for k in ("cols_ref", "weights_ref", "prev_ref", "last_ref")
        )
        held, ring, part_ref, sums = g["held"], g["ring"], g["part"], g["sums"]
        in_code, in_step, out_code, out_step = (
            g[k] for k in ("in_code", "in_step", "out_code", "out_step")
        )
        me = lax.axis_index("blk")
        eye = diagonal(wide, lanes)

        def load(c):
            slot = c % slots
            return pltpu.make_async_copy(
                g["values_ref"].at[pl.ds(c * batch, batch)], ring.at[slot], g["ring_sem"].at[slot]
            )

        def shard(d, src):
            return pltpu.make_async_copy(
                src, held.at[pl.ds(d * blocks, blocks)], g["held_sem"].at[d]
            )

        load(0).start()
        for d in range(n):

            @pl.when(me == d)
            def _(d=d):
                shard(d, g["own_ref"]).start()

            @pl.when(me != d)
            def _(d=d):
                shard(d, g["slab_ref"].at[pl.ds(d * blocks, blocks)]).start()

        if rest is not None:
            zs_copy = pltpu.make_async_copy(g["rest_ref"], g["zs"], g["zs_sem"])
            zs_copy.start()
        greet(me, n)
        sums[items] = jnp.zeros((wide, side), f32)

        @pl.when(me == 0)
        def _():
            in_step[0] = jnp.zeros((pieces, 1, lanes), f32)

        @pl.when(me == n - 1)
        def _():
            in_step[1] = jnp.zeros((pieces, 1, lanes), f32)

        extra = []
        ends = []
        if following is not None:
            step, steps, finish = gather_steps(
                me, n, 0, half, gather_size, g["following_ref"], g["following_slab_ref"],
                *(g[k] for k in early_names),
            )
            lead = min(2, steps)
            extra.append((lambda s, step=step: step(s + lead), steps - lead))
            ends.append(finish)
            for v in range(lead):
                step(v)
        if rest is not None:
            zs = g["zs"]

            def read_rest(d, c):
                return zs[pl.ds(d * late + c * late_size, late_size)]

            step, steps, finish = reduce_steps(
                me, n, late, late_size, eye, read_rest, zs, me * late,
                [g[k] for k in late_names], following is not None,
                max(half // gather_size - 2, 0) if following is not None else 0,
            )
            extra.append((step, steps))
            ends.append(finish)
            zs_copy.wait()

        for d in range(n):
            shard(d, g["own_ref"]).wait()

        def copies(way, c):
            to = {"blk": me + 1 - 2 * way}
            pairs = (
                (out_code, in_code, pl.ds(c * batch, batch)),
                (out_step, in_step, pl.ds(c, 1)),
            )
            return [
                pltpu.make_async_remote_copy(
                    src_ref=src.at[way, here],
                    dst_ref=dst.at[way, here],
                    send_sem=g["send_sem"].at[way, kind, c],
                    recv_sem=g["recv_sem"].at[way, kind, c],
                    device_id=to,
                    device_id_type=MESH,
                )
                for kind, (src, dst, here) in enumerate(pairs)
            ]

        def incoming(way, c):
            code = in_code[way, pl.ds(c * batch, batch)]
            return decode(code, in_step[way, pl.ds(c, 1)], eye)

        def relay(way, c, has, goes):
            @pl.when((c >= 0) & (c < pieces) & has)
            def _():
                for one in copies(way, c):
                    one.wait_recv()

            @pl.when((c >= 0) & (c < pieces) & goes)
            def _():
                at = pl.ds(c * batch, batch)
                code, step = encode(part_ref[at] + incoming(way, c), eye)
                out_code[way, at] = code
                out_step[way, pl.ds(c, 1)] = step
                for one in copies(way, c):
                    one.start()

        first_steps = max([pieces + lag] + [steps for _, steps in extra])
        if following is not None:
            late_step, late_steps, finish = gather_steps(
                me, n, half, late, late_size, g["following_ref"], g["following_slab_ref"],
                *(g[k] for k in after_names),
            )
            ends.append(finish)
            ahead = late // late_size

        @pl.loop(0, first_steps)
        def _(s):
            @pl.when(s + 1 < pieces)
            def _():
                load(s + 1).start()

            @pl.when(s < pieces)
            def _():
                load(s).wait()
                for r in range(batch):
                    total = None
                    for k in range(per):
                        at = (s * batch + r) * per + k
                        term = weights_ref[at] * lax.dot_general(
                            held[cols_ref[at]],
                            ring[s % slots, r, k],
                            (((1,), (1,)), ((), ())),
                            preferred_element_type=f32,
                        )
                        total = term if total is None else total + term
                    part_ref[s * batch + r] = total

            relay(0, s - HOP * me, me > 0, me < n - 1)
            relay(1, s - HOP * (n - 1 - me), me < n - 1, me > 0)
            for step, steps in extra:

                @pl.when(s < steps)
                def _(step=step):
                    step(s)

            if following is not None:

                @pl.when(s >= first_steps - ahead)
                def _():
                    late_step(s - (first_steps - ahead))

            c = s - lag

            @pl.when((c >= 0) & (c < pieces))
            def _():
                total = part_ref[pl.ds(c * batch, batch)] + incoming(0, c) + incoming(1, c)
                high = total.astype(jnp.bfloat16)
                low = (total - high.astype(f32)).astype(jnp.bfloat16)
                for r in range(batch):
                    both = jnp.concatenate([high[r], low[r]], axis=0)
                    for k in range(per):
                        at = (c * batch + r) * per + k
                        pair = lax.dot_general(
                            both,
                            ring[c % slots, r, k],
                            (((1,), (0,)), ((), ())),
                            preferred_element_type=f32,
                        )
                        term = weights_ref[at] * (pair[:wide] + pair[wide:])
                        sums[at] = term + sums[prev_ref[at]]

        if rest is not None:
            rest_copy = pltpu.make_async_copy(
                g["zs"].at[pl.ds(me * late, late)], g["rest_piece_ref"], g["zs_sem"]
            )
            rest_copy.start()

        mine = g["mine"]

        @pl.loop(0, now)
        def _(i):
            mine[i] = sums[last_ref[me * blocks + i]]

        def read_now(d, c):
            first = d * blocks + c * now_size
            return jnp.stack([sums[last_ref[first + i]] for i in range(now_size)])

        step, steps, finish = reduce_steps(
            me, n, now, now_size, eye, read_now, mine, 0, [g[k] for k in now_names],
            following is not None, 0,
        )
        second = [(step, steps)]
        ends.append(finish)
        if following is not None:
            second.append((lambda s: late_step(s + ahead), late_steps - ahead))
            shelf = g["shelf"]
            shelves = n * late // late_size
            per_shard = late // late_size

            def store(i):
                return pltpu.make_async_copy(
                    shelf.at[i % 2],
                    g["rest_out_ref"].at[pl.ds(i * late_size, late_size)],
                    g["shelf_sem"].at[i % 2],
                )

            def keep(i):
                @pl.when(i >= 2)
                def _():
                    store(i - 2).wait()

                first = i // per_shard * blocks + half + i % per_shard * late_size
                for j in range(late_size):
                    shelf[i % 2, j] = sums[last_ref[first + j]]
                store(i).start()

            second.append((keep, shelves))

        @pl.loop(0, max(steps for _, steps in second))
        def _(s):
            for step, steps in second:

                @pl.when(s < steps)
                def _(step=step):
                    step(s)

        mine_copies = [
            pltpu.make_async_copy(
                mine.at[pl.ds(a, b - a)], g[f"piece{i}_ref"], g["mine_sem"].at[i]
            )
            for i, (a, b) in enumerate(cuts)
        ]
        for one in mine_copies:
            one.start()

        @pl.loop(0, pieces)
        def _(c):
            @pl.when(me < n - 1)
            def _():
                for one in copies(0, c):
                    one.wait_send()

            @pl.when(me > 0)
            def _():
                for one in copies(1, c):
                    one.wait_send()

        for finish in ends:
            finish()
        if following is not None:
            for i in range(max(shelves - 2, 0), shelves):
                store(i).wait()
        if rest is not None:
            rest_copy.wait()
        for one in mine_copies:
            one.wait()

    results = pl.pallas_call(
        body,
        out_shape=list(outs.values()),
        in_specs=specs,
        out_specs=[ANY] * len(outs),
        scratch_shapes=list(scratch.values()),
        compiler_params=pltpu.CompilerParams(
            collective_id=2 + part, has_side_effects=True, vmem_limit_bytes=63 << 20
        ),
        name=f"stage_{part}",
    )(*args.values())
    return dict(zip(outs, results))


def factor(gram, total_rows):
    width = gram.shape[0]
    rounds = []
    for axis in ("row", "blk"):
        size = lax.axis_size(axis)
        if size & (size - 1):
            gram = lax.psum(gram, axis)
        else:
            rounds += [(axis, 1 << b) for b in range(size.bit_length() - 1)]
    count = len(rounds)
    f32 = jnp.float32

    def body(gram_ref, upper_ref, inverse_ref, sums, landed, left, right, send_sem, recv_sem):
        def partner(axis, bit):
            at = lax.axis_index(axis)
            return {axis: at + bit * (1 - 2 * (at // bit % 2))}

        barrier = pltpu.get_barrier_semaphore()
        for axis, bit in rounds:
            pl.semaphore_signal(barrier, inc=1, device_id=partner(axis, bit), device_id_type=MESH)
        pl.semaphore_wait(barrier, count)

        sums[0] = gram_ref[...]
        for i, (axis, bit) in enumerate(rounds):
            copy = pltpu.make_async_remote_copy(
                src_ref=sums.at[i],
                dst_ref=landed.at[i],
                send_sem=send_sem.at[i],
                recv_sem=recv_sem.at[i],
                device_id=partner(axis, bit),
                device_id_type=MESH,
            )
            copy.start()
            copy.wait()
            sums[i + 1] = sums[i] + landed[i]

        shape = (width, width)
        across = lax.broadcasted_iota(jnp.int32, shape, 0)
        along = lax.broadcasted_iota(jnp.int32, shape, 1)
        left[...] = sums[count] / total_rows
        right[...] = jnp.where(across == along, 1.0, 0.0)

        @pl.loop(0, width)
        def _(j):
            matrix = left[...]
            picked = along == j
            column = jnp.sum(jnp.where(picked, matrix, 0.0), axis=1, keepdims=True)
            row = left[pl.ds(j, 1)]
            other = right[pl.ds(j, 1)]
            pivot = jnp.sum(jnp.where(picked[:1], row, 0.0), axis=1, keepdims=True)
            scale = 1.0 / jnp.sqrt(pivot)
            row = row * scale
            other = other * scale
            column = jnp.where(across[:, :1] > j, column * scale, 0.0)
            here = across == j
            left[...] = jnp.where(here, row, matrix - column * row)
            right[...] = jnp.where(here, other, right[...] - column * other)

        upper_ref[...] = jnp.where(along >= across, left[...], 0.0)
        inverse_ref[...] = jnp.where(along <= across, right[...], 0.0)

    square = pltpu.VMEM((width, width), f32)
    return pl.pallas_call(
        body,
        out_shape=[jax.ShapeDtypeStruct((width, width), f32)] * 2,
        in_specs=[pl.BlockSpec(memory_space=pltpu.VMEM)],
        out_specs=[pl.BlockSpec(memory_space=pltpu.VMEM)] * 2,
        scratch_shapes=[
            pltpu.VMEM((count + 1, width, width), f32),
            pltpu.VMEM((count, width, width), f32),
            square,
            square,
            pltpu.SemaphoreType.DMA((count,)),
            pltpu.SemaphoreType.DMA((count,)),
        ],
        compiler_params=pltpu.CompilerParams(collective_id=30, has_side_effects=True),
        name="factor",
    )(gram)


def join(z_refs, early, b):
    here = [z_refs[2 * p + (0 if early else 1)][b] for p in range(len(z_refs) // 2)]
    return jnp.concatenate(here, axis=0)


def block_specs(pieces, batch, early_steps):
    specs = []
    for i, piece in enumerate(pieces):
        shape = (batch,) + piece.shape[1:]
        if i % 2 == 0:
            specs.append(pl.BlockSpec(shape, lambda i: (jnp.minimum(i, early_steps - 1), 0, 0)))
        else:
            specs.append(pl.BlockSpec(shape, lambda i: (jnp.maximum(i - early_steps, 0), 0, 0)))
    return specs


def halves(x):
    high = x.astype(jnp.bfloat16)
    return high, (x - high.astype(jnp.float32)).astype(jnp.bfloat16)


def outer(x, y):
    return lax.dot_general(x, y, (((1,), (1,)), ((), ())), preferred_element_type=jnp.float32)


def gram_of(pieces):
    early, late = pieces[0].shape[0], pieces[1].shape[0]
    side = pieces[0].shape[2]
    width = sum(piece.shape[1] for piece in pieces[::2])
    batch = divisor(math.gcd(early, late), 8)

    def body(*refs):
        *z_refs, out_ref, total = refs

        @pl.when(pl.program_id(0) == 0)
        def _():
            total[...] = jnp.zeros_like(total)

        for first in (True, False):

            @pl.when((pl.program_id(0) < early // batch) == first)
            def _(first=first):
                part = None
                for b in range(batch):
                    high, low = halves(join(z_refs, first, b))
                    term = outer(jnp.concatenate([high, low], axis=0), high)
                    part = term if part is None else part + term
                total[...] += part

        @pl.when(pl.program_id(0) == pl.num_programs(0) - 1)
        def _():
            cross = total[width:]
            out_ref[...] = total[:width] + (cross + cross.T)

    return pl.pallas_call(
        body,
        out_shape=jax.ShapeDtypeStruct((width, width), jnp.float32),
        grid=((early + late) // batch,),
        in_specs=block_specs(pieces, batch, early // batch),
        out_specs=pl.BlockSpec((width, width), lambda i: (0, 0)),
        scratch_shapes=[pltpu.VMEM((2 * width, width), jnp.float32)],
        name="gram",
    )(*pieces)


def crossed(x, y):
    return lax.dot_general(x, y, (((0,), (1,)), ((), ())), preferred_element_type=jnp.float32)


def solve(pieces, inverse):
    early, late = pieces[0].shape[0], pieces[1].shape[0]
    side = pieces[0].shape[2]
    width = sum(piece.shape[1] for piece in pieces[::2])
    batch = divisor(math.gcd(early, late), 8)

    def body(*refs):
        *z_refs, inverse_ref, out_ref = refs
        inv_high, inv_low = halves(inverse_ref[...])
        inv_twice = jnp.concatenate([inv_high, inv_high], axis=1)
        for first in (True, False):

            @pl.when((pl.program_id(0) < early // batch) == first)
            def _(first=first):
                for b in range(batch):
                    high, low = halves(join(z_refs, first, b))
                    both = jnp.concatenate([high, low], axis=0)
                    out_ref[b] = crossed(both, inv_twice) + crossed(high, inv_low)

    return pl.pallas_call(
        body,
        out_shape=jax.ShapeDtypeStruct((early + late, side, width), jnp.float32),
        grid=((early + late) // batch,),
        in_specs=block_specs(pieces, batch, early // batch)
        + [pl.BlockSpec((width, width), lambda i: (0, 0))],
        out_specs=pl.BlockSpec((batch, side, width), lambda i: (i, 0, 0)),
        name="solve",
    )(*pieces, inverse)


def local(values, scales, pattern, omega):
    rows, per = pattern.shape
    blocks, side, width = omega.shape
    n = lax.axis_size("blk")
    items = rows * per
    columns = blocks * n
    cols = pattern.reshape(-1) - lax.axis_index("row") * columns
    weights = scales.astype(jnp.float32).reshape(-1)
    slot = jnp.arange(items)
    same = cols[:, None] == cols[None, :]
    prev = jnp.max(jnp.where(same & (slot[None, :] < slot[:, None]), slot[None, :], -1), axis=1)
    prev = jnp.where(prev < 0, items, prev)
    hits = jnp.arange(columns)[:, None] == cols[None, :]
    last = jnp.max(jnp.where(hits, slot[None, :], -1), axis=1)
    last = jnp.where(last < 0, items, last)

    parts = 4
    slab, *own = gather(omega, n, parts)
    rest = None
    pieces = []
    for p in range(parts):
        following = own[p + 1] if p + 1 < parts else None
        done = stage(p, values, own[p], slab, (cols, weights, prev, last), n, following, rest)
        if p:
            pieces.append(done["rest_piece"])
        if p + 1 < parts:
            pieces.append(done["piece0"])
            slab, rest = done["following_slab"], done["rest_out"]
        else:
            pieces += [done["piece0"], done["piece1"]]

    total_rows = columns * side * lax.axis_size("row")
    upper, inverse = factor(gram_of(pieces), total_rows)
    return solve(pieces, inverse), upper


def solution(mesh):
    return jax.shard_map(
        local,
        mesh=mesh,
        in_specs=(
            P("row", "blk", None, None),
            P("row", "blk"),
            P("row", "blk"),
            P(("row", "blk"), None, None),
        ),
        out_specs=(P(("row", "blk"), None, None), P()),
        check_vma=False,
    )
```

```python
import math

import jax
import jax.numpy as jnp
from jax import lax
from jax.experimental import pallas as pl
from jax.experimental.pallas import tpu as pltpu
from jax.sharding import PartitionSpec as P

MESH = pl.DeviceIdType.MESH
LEVELS = 32767.0
TINY = 1e-30
HOP = 2
ANY = pl.BlockSpec(memory_space=pl.ANY)
SMEM = pl.BlockSpec(memory_space=pltpu.SMEM)


def divisor(n, most):
    return max(d for d in range(1, most + 1) if n % d == 0)


def diagonal(height, width):
    shape = (height, width)
    return lax.broadcasted_iota(jnp.int32, shape, 0) == lax.broadcasted_iota(jnp.int32, shape, 1)


def encode(x, eye):
    peak = jnp.max(jnp.max(jnp.abs(x), axis=0, keepdims=True), axis=2, keepdims=True)
    live = peak > TINY
    inverse = jnp.where(live, LEVELS / jnp.where(live, peak, 1.0), 0.0)
    code = jnp.round(x * inverse).astype(jnp.int32).astype(jnp.int16)
    step = jnp.sum(jnp.where(eye[None], peak * (1.0 / LEVELS), 0.0), axis=1, keepdims=True)
    return code, step


def decode(code, step, eye):
    column = jnp.sum(jnp.where(eye[None], step, 0.0), axis=2, keepdims=True)
    return code.astype(jnp.int32).astype(jnp.float32) * column


def greet(me, n):
    barrier = pltpu.get_barrier_semaphore()

    @pl.when(me > 0)
    def _():
        pl.semaphore_signal(barrier, inc=1, device_id={"blk": me - 1}, device_id_type=MESH)

    @pl.when(me < n - 1)
    def _():
        pl.semaphore_signal(barrier, inc=1, device_id={"blk": me + 1}, device_id_type=MESH)

    peers = jnp.where(me > 0, 1, 0) + jnp.where(me < n - 1, 1, 0)
    pl.semaphore_wait(barrier, peers)


def gather_steps(me, n, base, count, size, own_ref, slab_ref, send_sem, recv_sem):
    blocks = own_ref.shape[0]
    pieces = count // size

    def copy(way, t, c, owner):
        here = slab_ref.at[pl.ds(owner * blocks + base + c * size, size)]
        return pltpu.make_async_remote_copy(
            src_ref=here,
            dst_ref=here,
            send_sem=send_sem.at[way, t, c],
            recv_sem=recv_sem.at[way, t, c],
            device_id={"blk": me + 1 - 2 * way},
            device_id_type=MESH,
        )

    def first(way, c):
        return pltpu.make_async_remote_copy(
            src_ref=own_ref.at[pl.ds(base + c * size, size)],
            dst_ref=slab_ref.at[pl.ds(me * blocks + base + c * size, size)],
            send_sem=send_sem.at[way, 0, c],
            recv_sem=recv_sem.at[way, 0, c],
            device_id={"blk": me + 1 - 2 * way},
            device_id_type=MESH,
        )

    def has(way, t):
        behind = me if way == 0 else n - 1 - me
        return behind >= t

    def goes(way):
        return me < n - 1 if way == 0 else me > 0

    def owner_of(way, t):
        return me - t if way == 0 else me + t

    def step(v):
        t = v // pieces
        c = v % pieces
        for way in (0, 1):

            @pl.when((t == 0) & goes(way))
            def _(way=way):
                first(way, c).start()

            @pl.when((t > 0) & has(way, t))
            def _(way=way):
                copy(way, t - 1, c, owner_of(way, t)).wait_recv()

            @pl.when((t > 0) & (t < n - 1) & has(way, t) & goes(way))
            def _(way=way):
                copy(way, t, c, owner_of(way, t)).start()

    def finish():
        @pl.loop(0, (n - 1) * pieces)
        def _(v):
            t = v // pieces
            c = v % pieces
            for way in (0, 1):

                @pl.when(has(way, t) & goes(way))
                def _(way=way):
                    copy(way, t, c, me).wait_send()

    return step, n * pieces, finish


def gather_sems(n, count, size):
    return [pltpu.SemaphoreType.DMA((2, n - 1, count // size))] * 2


def gather(omega, n, parts):
    blocks, side, width = omega.shape
    wide = width // parts
    size = divisor(blocks, 4)
    pieces = blocks // size

    def body(omega_ref, *refs):
        slab_ref, *own_refs = refs[: 1 + parts]
        raw, turned, raw_sem, own_sem, *sems = refs[1 + parts :]
        me = lax.axis_index("blk")

        def load(c):
            at = pl.ds(c * size, size)
            return pltpu.make_async_copy(omega_ref.at[at], raw.at[at], raw_sem.at[c])

        def keep(p, c):
            at = pl.ds(c * size, size)
            return pltpu.make_async_copy(turned.at[p, at], own_refs[p].at[at], own_sem.at[p, c])

        for c in range(pieces):
            load(c).start()
        greet(me, n)
        step, steps, finish = gather_steps(me, n, 0, blocks, size, turned.at[0], slab_ref, *sems)

        @pl.loop(0, steps)
        def _(s):
            @pl.when(s < pieces)
            def _():
                load(s).wait()
                for i in range(size):
                    block = raw[s * size + i].T
                    for p in range(parts):
                        turned[p, s * size + i] = block[p * wide : (p + 1) * wide]

            step(s)

            @pl.when(s < pieces)
            def _():
                for p in range(parts):
                    keep(p, s).start()

        finish()

        @pl.loop(0, pieces)
        def _(c):
            for p in range(parts):
                keep(p, c).wait()

    return pl.pallas_call(
        body,
        out_shape=[jax.ShapeDtypeStruct((n * blocks, wide, side), omega.dtype)]
        + [jax.ShapeDtypeStruct((blocks, wide, side), omega.dtype)] * parts,
        in_specs=[ANY],
        out_specs=[ANY] * (1 + parts),
        scratch_shapes=[
            pltpu.VMEM(omega.shape, omega.dtype),
            pltpu.VMEM((parts, blocks, wide, side), omega.dtype),
            pltpu.SemaphoreType.DMA((pieces,)),
            pltpu.SemaphoreType.DMA((parts, pieces)),
        ]
        + gather_sems(n, blocks, size),
        compiler_params=pltpu.CompilerParams(collective_id=1, has_side_effects=True),
        name="gather",
    )(omega)


def reduce_scratch(n, count, size, wide, side, lanes):
    far = (n - 1) * count
    sems = pltpu.SemaphoreType.DMA((2, 2, far // size))
    code = pltpu.VMEM((2, far, wide, side), jnp.int16)
    step = pltpu.VMEM((2, far // size, 1, lanes), jnp.float32)
    return [code, step, code, step, sems, sems]


def reduce_steps(me, n, count, size, eye, read, total, base, scratch, beside, start):
    in_code, in_step, out_code, out_step, send_sem, recv_sem = scratch
    pieces = count // size
    reach = (n - 1) * pieces
    far = ((n - 1 - me) * pieces, me * pieces)
    hop = max(pieces, HOP) if beside else HOP

    def copies(way, u):
        to = {"blk": me + 1 - 2 * way}
        pairs = (out_code, in_code, pl.ds(u * size, size)), (out_step, in_step, pl.ds(u, 1))
        return [
            pltpu.make_async_remote_copy(
                src_ref=src.at[way, here],
                dst_ref=dst.at[way, here],
                send_sem=send_sem.at[way, kind, u],
                recv_sem=recv_sem.at[way, kind, u],
                device_id=to,
                device_id_type=MESH,
            )
            for kind, (src, dst, here) in enumerate(pairs)
        ]

    def incoming(way, u):
        return decode(in_code[way, pl.ds(u * size, size)], in_step[way, pl.ds(u, 1)], eye)

    def push(way, u, value):
        code, step = encode(value, eye)
        out_code[way, pl.ds(u * size, size)] = code
        out_step[way, pl.ds(u, 1)] = step
        for one in copies(way, u):
            one.start()

    def source(way, u):
        d = n - 1 - u // pieces if way == 0 else u // pieces
        return read(d, u % pieces)

    def step(s):
        for way in (0, 1):
            behind = me if way == 0 else n - 1 - me
            u = s - start - hop * behind
            inside = (u >= 0) & (u < far[way])

            @pl.when(inside & (behind == 0))
            def _(way=way, u=u):
                push(way, u, source(way, u))

            @pl.when(inside & (behind > 0))
            def _(way=way, u=u):
                for one in copies(way, u):
                    one.wait_recv()
                push(way, u, source(way, u) + incoming(way, u))

            @pl.when((behind > 0) & (u >= far[way]) & (u < far[way] + pieces))
            def _(way=way, u=u):
                for one in copies(way, u):
                    one.wait_recv()
                at = pl.ds(base + (u - far[way]) * size, size)
                total[at] = total[at] + incoming(way, u)

    def finish():
        @pl.loop(0, reach)
        def _(u):
            for way in (0, 1):

                @pl.when(u < far[way])
                def _(way=way):
                    for one in copies(way, u):
                        one.wait_send()

    return step, start + max([reach] + [hop * b + (n - b) * pieces for b in range(1, n)]), finish


def stage(part, values, own, slab, tables, n, following=None, rest=None):
    rows, per, side, _ = values.shape
    blocks, wide, _ = own.shape
    lanes = 128
    items = rows * per
    columns = n * blocks
    batch = divisor(rows, 4)
    pieces = rows // batch
    lag = HOP * (n - 1)
    slots = lag + 2
    half = blocks // 2
    late = blocks - half
    now = half if following is not None else blocks
    now_size = divisor(now, 4 if following is not None else 8)
    late_size = divisor(late, 4)
    gather_size = divisor(half, 4)
    f32 = jnp.float32

    args = dict(zip(("cols", "weights", "prev", "last"), tables))
    args.update(values=values, own=own, slab=slab)
    specs = [SMEM] * 4 + [ANY] * 3
    cuts = [(0, half)] + ([(half, blocks)] if following is None else [])
    outs = {
        f"piece{i}": jax.ShapeDtypeStruct((b - a, wide, side), f32) for i, (a, b) in enumerate(cuts)
    }
    scratch = dict(
        held=pltpu.VMEM((columns, wide, side), own.dtype),
        ring=pltpu.VMEM((slots, batch, per, side, side), values.dtype),
        part=pltpu.VMEM((rows, wide, side), f32),
        in_code=pltpu.VMEM((2, rows, wide, side), jnp.int16),
        in_step=pltpu.VMEM((2, pieces, 1, lanes), f32),
        out_code=pltpu.VMEM((2, rows, wide, side), jnp.int16),
        out_step=pltpu.VMEM((2, pieces, 1, lanes), f32),
        sums=pltpu.VMEM((items + 1, wide, side), f32),
        mine=pltpu.VMEM((now, wide, side), f32),
        held_sem=pltpu.SemaphoreType.DMA((n,)),
        ring_sem=pltpu.SemaphoreType.DMA((slots,)),
        send_sem=pltpu.SemaphoreType.DMA((2, 2, pieces)),
        recv_sem=pltpu.SemaphoreType.DMA((2, 2, pieces)),
        mine_sem=pltpu.SemaphoreType.DMA((len(cuts),)),
    )

    def group(name, shapes):
        scratch.update({f"{name}{i}": shape for i, shape in enumerate(shapes)})
        return [f"{name}{i}" for i in range(len(shapes))]

    now_names = group("now", reduce_scratch(n, now, now_size, wide, side, lanes))
    if following is not None:
        args.update(following=following)
        specs.append(ANY)
        outs.update(
            following_slab=jax.ShapeDtypeStruct(slab.shape, slab.dtype),
            rest_out=jax.ShapeDtypeStruct((n * late, wide, side), f32),
        )
        early_names = group("early", gather_sems(n, half, gather_size))
        after_names = group("after", gather_sems(n, late, late_size))
        scratch.update(
            shelf=pltpu.VMEM((2, late_size, wide, side), f32),
            shelf_sem=pltpu.SemaphoreType.DMA((2,)),
        )
    if rest is not None:
        args.update(rest=rest)
        specs.append(ANY)
        outs.update(rest_piece=jax.ShapeDtypeStruct((late, wide, side), f32))
        late_names = group("late", reduce_scratch(n, late, late_size, wide, side, lanes))
        scratch.update(
            zs=pltpu.VMEM((n * late, wide, side), f32),
            zs_sem=pltpu.SemaphoreType.DMA(()),
        )
    names = list(args) + list(outs) + list(scratch)
    names[len(args) : len(args) + len(outs)] = [f"{name}_ref" for name in outs]
    names[: len(args)] = [f"{name}_ref" for name in args]

    def body(*refs):
        g = dict(zip(names, refs, strict=True))
        cols_ref, weights_ref, prev_ref, last_ref = (
            g[k] for k in ("cols_ref", "weights_ref", "prev_ref", "last_ref")
        )
        held, ring, part_ref, sums = g["held"], g["ring"], g["part"], g["sums"]
        in_code, in_step, out_code, out_step = (
            g[k] for k in ("in_code", "in_step", "out_code", "out_step")
        )
        me = lax.axis_index("blk")
        eye = diagonal(wide, lanes)

        def load(c):
            slot = c % slots
            return pltpu.make_async_copy(
                g["values_ref"].at[pl.ds(c * batch, batch)], ring.at[slot], g["ring_sem"].at[slot]
            )

        def shard(d, src):
            return pltpu.make_async_copy(
                src, held.at[pl.ds(d * blocks, blocks)], g["held_sem"].at[d]
            )

        load(0).start()
        for d in range(n):

            @pl.when(me == d)
            def _(d=d):
                shard(d, g["own_ref"]).start()

            @pl.when(me != d)
            def _(d=d):
                shard(d, g["slab_ref"].at[pl.ds(d * blocks, blocks)]).start()

        if rest is not None:
            zs_copy = pltpu.make_async_copy(g["rest_ref"], g["zs"], g["zs_sem"])
            zs_copy.start()
        greet(me, n)
        sums[items] = jnp.zeros((wide, side), f32)

        @pl.when(me == 0)
        def _():
            in_step[0] = jnp.zeros((pieces, 1, lanes), f32)

        @pl.when(me == n - 1)
        def _():
            in_step[1] = jnp.zeros((pieces, 1, lanes), f32)

        extra = []
        ends = []
        if following is not None:
            step, steps, finish = gather_steps(
                me, n, 0, half, gather_size, g["following_ref"], g["following_slab_ref"],
                *(g[k] for k in early_names),
            )
            lead = min(2, steps)
            extra.append((lambda s, step=step: step(s + lead), steps - lead))
            ends.append(finish)
            for v in range(lead):
                step(v)
        if rest is not None:
            zs = g["zs"]

            def read_rest(d, c):
                return zs[pl.ds(d * late + c * late_size, late_size)]

            step, steps, finish = reduce_steps(
                me, n, late, late_size, eye, read_rest, zs, me * late,
                [g[k] for k in late_names], following is not None,
                max(half // gather_size - 2, 0) if following is not None else 0,
            )
            extra.append((step, steps))
            ends.append(finish)
            zs_copy.wait()

        for d in range(n):
            shard(d, g["own_ref"]).wait()

        def copies(way, c):
            to = {"blk": me + 1 - 2 * way}
            pairs = (
                (out_code, in_code, pl.ds(c * batch, batch)),
                (out_step, in_step, pl.ds(c, 1)),
            )
            return [
                pltpu.make_async_remote_copy(
                    src_ref=src.at[way, here],
                    dst_ref=dst.at[way, here],
                    send_sem=g["send_sem"].at[way, kind, c],
                    recv_sem=g["recv_sem"].at[way, kind, c],
                    device_id=to,
                    device_id_type=MESH,
                )
                for kind, (src, dst, here) in enumerate(pairs)
            ]

        def incoming(way, c):
            code = in_code[way, pl.ds(c * batch, batch)]
            return decode(code, in_step[way, pl.ds(c, 1)], eye)

        def relay(way, c, has, goes):
            @pl.when((c >= 0) & (c < pieces) & has)
            def _():
                for one in copies(way, c):
                    one.wait_recv()

            @pl.when((c >= 0) & (c < pieces) & goes)
            def _():
                at = pl.ds(c * batch, batch)
                code, step = encode(part_ref[at] + incoming(way, c), eye)
                out_code[way, at] = code
                out_step[way, pl.ds(c, 1)] = step
                for one in copies(way, c):
                    one.start()

        first_steps = max([pieces + lag] + [steps for _, steps in extra])
        if following is not None:
            late_step, late_steps, finish = gather_steps(
                me, n, half, late, late_size, g["following_ref"], g["following_slab_ref"],
                *(g[k] for k in after_names),
            )
            ends.append(finish)
            ahead = late // late_size

        @pl.loop(0, first_steps)
        def _(s):
            @pl.when(s + 1 < pieces)
            def _():
                load(s + 1).start()

            @pl.when(s < pieces)
            def _():
                load(s).wait()
                for r in range(batch):
                    total = None
                    for k in range(per):
                        at = (s * batch + r) * per + k
                        term = weights_ref[at] * lax.dot_general(
                            held[cols_ref[at]],
                            ring[s % slots, r, k],
                            (((1,), (1,)), ((), ())),
                            preferred_element_type=f32,
                        )
                        total = term if total is None else total + term
                    part_ref[s * batch + r] = total

            relay(0, s - HOP * me, me > 0, me < n - 1)
            relay(1, s - HOP * (n - 1 - me), me < n - 1, me > 0)
            for step, steps in extra:

                @pl.when(s < steps)
                def _(step=step):
                    step(s)

            if following is not None:

                @pl.when(s >= first_steps - ahead)
                def _():
                    late_step(s - (first_steps - ahead))

            c = s - lag

            @pl.when((c >= 0) & (c < pieces))
            def _():
                total = part_ref[pl.ds(c * batch, batch)] + incoming(0, c) + incoming(1, c)
                high = total.astype(jnp.bfloat16)
                low = (total - high.astype(f32)).astype(jnp.bfloat16)
                for r in range(batch):
                    both = jnp.concatenate([high[r], low[r]], axis=0)
                    for k in range(per):
                        at = (c * batch + r) * per + k
                        pair = lax.dot_general(
                            both,
                            ring[c % slots, r, k],
                            (((1,), (0,)), ((), ())),
                            preferred_element_type=f32,
                        )
                        term = weights_ref[at] * (pair[:wide] + pair[wide:])
                        sums[at] = term + sums[prev_ref[at]]

        if rest is not None:
            rest_copy = pltpu.make_async_copy(
                g["zs"].at[pl.ds(me * late, late)], g["rest_piece_ref"], g["zs_sem"]
            )
            rest_copy.start()

        mine = g["mine"]

        @pl.loop(0, now)
        def _(i):
            mine[i] = sums[last_ref[me * blocks + i]]

        def read_now(d, c):
            first = d * blocks + c * now_size
            return jnp.stack([sums[last_ref[first + i]] for i in range(now_size)])

        step, steps, finish = reduce_steps(
            me, n, now, now_size, eye, read_now, mine, 0, [g[k] for k in now_names],
            following is not None, 0,
        )
        second = [(step, steps)]
        ends.append(finish)
        if following is not None:
            second.append((lambda s: late_step(s + ahead), late_steps - ahead))
            shelf = g["shelf"]
            shelves = n * late // late_size
            per_shard = late // late_size

            def store(i):
                return pltpu.make_async_copy(
                    shelf.at[i % 2],
                    g["rest_out_ref"].at[pl.ds(i * late_size, late_size)],
                    g["shelf_sem"].at[i % 2],
                )

            def keep(i):
                @pl.when(i >= 2)
                def _():
                    store(i - 2).wait()

                first = i // per_shard * blocks + half + i % per_shard * late_size
                for j in range(late_size):
                    shelf[i % 2, j] = sums[last_ref[first + j]]
                store(i).start()

            second.append((keep, shelves))

        @pl.loop(0, max(steps for _, steps in second))
        def _(s):
            for step, steps in second:

                @pl.when(s < steps)
                def _(step=step):
                    step(s)

        mine_copies = [
            pltpu.make_async_copy(
                mine.at[pl.ds(a, b - a)], g[f"piece{i}_ref"], g["mine_sem"].at[i]
            )
            for i, (a, b) in enumerate(cuts)
        ]
        for one in mine_copies:
            one.start()

        @pl.loop(0, pieces)
        def _(c):
            @pl.when(me < n - 1)
            def _():
                for one in copies(0, c):
                    one.wait_send()

            @pl.when(me > 0)
            def _():
                for one in copies(1, c):
                    one.wait_send()

        for finish in ends:
            finish()
        if following is not None:
            for i in range(max(shelves - 2, 0), shelves):
                store(i).wait()
        if rest is not None:
            rest_copy.wait()
        for one in mine_copies:
            one.wait()

    results = pl.pallas_call(
        body,
        out_shape=list(outs.values()),
        in_specs=specs,
        out_specs=[ANY] * len(outs),
        scratch_shapes=list(scratch.values()),
        compiler_params=pltpu.CompilerParams(
            collective_id=2 + part, has_side_effects=True, vmem_limit_bytes=63 << 20
        ),
        name=f"stage_{part}",
    )(*args.values())
    return dict(zip(outs, results))


def factor(gram, total_rows):
    width = gram.shape[0]
    rounds = []
    for axis in ("row", "blk"):
        size = lax.axis_size(axis)
        if size & (size - 1):
            gram = lax.psum(gram, axis)
        else:
            rounds += [(axis, 1 << b) for b in range(size.bit_length() - 1)]
    count = len(rounds)
    f32 = jnp.float32

    def body(gram_ref, upper_ref, inverse_ref, sums, landed, left, right, send_sem, recv_sem):
        def partner(axis, bit):
            at = lax.axis_index(axis)
            return {axis: at + bit * (1 - 2 * (at // bit % 2))}

        barrier = pltpu.get_barrier_semaphore()
        for axis, bit in rounds:
            pl.semaphore_signal(barrier, inc=1, device_id=partner(axis, bit), device_id_type=MESH)
        pl.semaphore_wait(barrier, count)

        sums[0] = gram_ref[...]
        for i, (axis, bit) in enumerate(rounds):
            copy = pltpu.make_async_remote_copy(
                src_ref=sums.at[i],
                dst_ref=landed.at[i],
                send_sem=send_sem.at[i],
                recv_sem=recv_sem.at[i],
                device_id=partner(axis, bit),
                device_id_type=MESH,
            )
            copy.start()
            copy.wait()
            sums[i + 1] = sums[i] + landed[i]

        shape = (width, width)
        across = lax.broadcasted_iota(jnp.int32, shape, 0)
        along = lax.broadcasted_iota(jnp.int32, shape, 1)
        left[...] = sums[count] / total_rows
        right[...] = jnp.where(across == along, 1.0, 0.0)

        panel = divisor(width, 8)
        down = lax.broadcasted_iota(jnp.int32, (panel, width), 0)
        over = lax.broadcasted_iota(jnp.int32, (panel, width), 1)

        @pl.loop(0, width // panel)
        def _(q):
            first = pl.multiple_of(q * panel, panel)
            here = pl.ds(first, panel)
            rows = [left[here], right[here]]
            columns = [
                jnp.broadcast_to(
                    jnp.sum(jnp.where(over == first + t, rows[0], 0.0), axis=1, keepdims=True),
                    (panel, width),
                )
                for t in range(panel)
            ]
            for t in range(panel):
                scale = 1.0 / jnp.sqrt(columns[t][t : t + 1])
                factors = jnp.where(down > t, columns[t] * scale, 0.0)

                def pass_on(x, t=t, scale=scale, factors=factors):
                    row = x[t : t + 1] * scale
                    return jnp.where(down == t, row, x - factors * row)

                columns = [pass_on(x) if u > t else x for u, x in enumerate(columns)]
                rows = [pass_on(x) for x in rows]
            below = jnp.where(along[:1] >= first + panel, rows[0], 0.0)
            left[here] = rows[0]
            right[here] = rows[1]
            change = lax.dot_general(
                below,
                jnp.concatenate(rows, axis=1),
                (((0,), (0,)), ((), ())),
                precision=lax.Precision.HIGHEST,
                preferred_element_type=f32,
            )
            left[...] = left[...] - change[:, :width]
            right[...] = right[...] - change[:, width:]

        upper_ref[...] = jnp.where(along >= across, left[...], 0.0)
        inverse_ref[...] = jnp.where(along <= across, right[...], 0.0)

    square = pltpu.VMEM((width, width), f32)
    return pl.pallas_call(
        body,
        out_shape=[jax.ShapeDtypeStruct((width, width), f32)] * 2,
        in_specs=[pl.BlockSpec(memory_space=pltpu.VMEM)],
        out_specs=[pl.BlockSpec(memory_space=pltpu.VMEM)] * 2,
        scratch_shapes=[
            pltpu.VMEM((count + 1, width, width), f32),
            pltpu.VMEM((count, width, width), f32),
            square,
            square,
            pltpu.SemaphoreType.DMA((count,)),
            pltpu.SemaphoreType.DMA((count,)),
        ],
        compiler_params=pltpu.CompilerParams(collective_id=30, has_side_effects=True),
        name="factor",
    )(gram)


def join(z_refs, early, b):
    here = [z_refs[2 * p + (0 if early else 1)][b] for p in range(len(z_refs) // 2)]
    return jnp.concatenate(here, axis=0)


def block_specs(pieces, batch, early_steps):
    specs = []
    for i, piece in enumerate(pieces):
        shape = (batch,) + piece.shape[1:]
        if i % 2 == 0:
            specs.append(pl.BlockSpec(shape, lambda i: (jnp.minimum(i, early_steps - 1), 0, 0)))
        else:
            specs.append(pl.BlockSpec(shape, lambda i: (jnp.maximum(i - early_steps, 0), 0, 0)))
    return specs


def halves(x):
    high = x.astype(jnp.bfloat16)
    return high, (x - high.astype(jnp.float32)).astype(jnp.bfloat16)


def outer(x, y):
    return lax.dot_general(x, y, (((1,), (1,)), ((), ())), preferred_element_type=jnp.float32)


def gram_of(pieces):
    early, late = pieces[0].shape[0], pieces[1].shape[0]
    side = pieces[0].shape[2]
    width = sum(piece.shape[1] for piece in pieces[::2])
    batch = divisor(math.gcd(early, late), 8)

    def body(*refs):
        *z_refs, out_ref, total = refs

        @pl.when(pl.program_id(0) == 0)
        def _():
            total[...] = jnp.zeros_like(total)

        for first in (True, False):

            @pl.when((pl.program_id(0) < early // batch) == first)
            def _(first=first):
                part = None
                for b in range(batch):
                    high, low = halves(join(z_refs, first, b))
                    term = outer(jnp.concatenate([high, low], axis=0), high)
                    part = term if part is None else part + term
                total[...] += part

        @pl.when(pl.program_id(0) == pl.num_programs(0) - 1)
        def _():
            cross = total[width:]
            out_ref[...] = total[:width] + (cross + cross.T)

    return pl.pallas_call(
        body,
        out_shape=jax.ShapeDtypeStruct((width, width), jnp.float32),
        grid=((early + late) // batch,),
        in_specs=block_specs(pieces, batch, early // batch),
        out_specs=pl.BlockSpec((width, width), lambda i: (0, 0)),
        scratch_shapes=[pltpu.VMEM((2 * width, width), jnp.float32)],
        name="gram",
    )(*pieces)


def crossed(x, y):
    return lax.dot_general(x, y, (((0,), (1,)), ((), ())), preferred_element_type=jnp.float32)


def solve(pieces, inverse):
    early, late = pieces[0].shape[0], pieces[1].shape[0]
    side = pieces[0].shape[2]
    width = sum(piece.shape[1] for piece in pieces[::2])
    batch = divisor(math.gcd(early, late), 8)

    def body(*refs):
        *z_refs, inverse_ref, out_ref = refs
        inv_high, inv_low = halves(inverse_ref[...])
        inv_twice = jnp.concatenate([inv_high, inv_high], axis=1)
        for first in (True, False):

            @pl.when((pl.program_id(0) < early // batch) == first)
            def _(first=first):
                for b in range(batch):
                    high, low = halves(join(z_refs, first, b))
                    both = jnp.concatenate([high, low], axis=0)
                    out_ref[b] = crossed(both, inv_twice) + crossed(high, inv_low)

    return pl.pallas_call(
        body,
        out_shape=jax.ShapeDtypeStruct((early + late, side, width), jnp.float32),
        grid=((early + late) // batch,),
        in_specs=block_specs(pieces, batch, early // batch)
        + [pl.BlockSpec((width, width), lambda i: (0, 0))],
        out_specs=pl.BlockSpec((batch, side, width), lambda i: (i, 0, 0)),
        name="solve",
    )(*pieces, inverse)


def local(values, scales, pattern, omega):
    rows, per = pattern.shape
    blocks, side, width = omega.shape
    n = lax.axis_size("blk")
    items = rows * per
    columns = blocks * n
    cols = pattern.reshape(-1) - lax.axis_index("row") * columns
    weights = scales.astype(jnp.float32).reshape(-1)
    slot = jnp.arange(items)
    same = cols[:, None] == cols[None, :]
    prev = jnp.max(jnp.where(same & (slot[None, :] < slot[:, None]), slot[None, :], -1), axis=1)
    prev = jnp.where(prev < 0, items, prev)
    hits = jnp.arange(columns)[:, None] == cols[None, :]
    last = jnp.max(jnp.where(hits, slot[None, :], -1), axis=1)
    last = jnp.where(last < 0, items, last)

    parts = 4
    slab, *own = gather(omega, n, parts)
    rest = None
    pieces = []
    for p in range(parts):
        following = own[p + 1] if p + 1 < parts else None
        done = stage(p, values, own[p], slab, (cols, weights, prev, last), n, following, rest)
        if p:
            pieces.append(done["rest_piece"])
        if p + 1 < parts:
            pieces.append(done["piece0"])
            slab, rest = done["following_slab"], done["rest_out"]
        else:
            pieces += [done["piece0"], done["piece1"]]

    total_rows = columns * side * lax.axis_size("row")
    upper, inverse = factor(gram_of(pieces), total_rows)
    return solve(pieces, inverse), upper


def solution(mesh):
    return jax.shard_map(
        local,
        mesh=mesh,
        in_specs=(
            P("row", "blk", None, None),
            P("row", "blk"),
            P("row", "blk"),
            P(("row", "blk"), None, None),
        ),
        out_specs=(P(("row", "blk"), None, None), P()),
        check_vma=False,
    )
```

```python
import math

import jax
import jax.numpy as jnp
from jax import lax
from jax.experimental import pallas as pl
from jax.experimental.pallas import tpu as pltpu
from jax.sharding import PartitionSpec as P

MESH = pl.DeviceIdType.MESH
LEVELS = 32767.0
TINY = 1e-30
HOP = 2
LEAD = 8
ANY = pl.BlockSpec(memory_space=pl.ANY)
SMEM = pl.BlockSpec(memory_space=pltpu.SMEM)


def divisor(n, most):
    return max(d for d in range(1, most + 1) if n % d == 0)


def diagonal(height, width):
    shape = (height, width)
    return lax.broadcasted_iota(jnp.int32, shape, 0) == lax.broadcasted_iota(jnp.int32, shape, 1)


def encode(x, eye):
    peak = jnp.max(jnp.max(jnp.abs(x), axis=0, keepdims=True), axis=2, keepdims=True)
    live = peak > TINY
    inverse = jnp.where(live, LEVELS / jnp.where(live, peak, 1.0), 0.0)
    code = jnp.round(x * inverse).astype(jnp.int32).astype(jnp.int16)
    step = jnp.sum(jnp.where(eye[None], peak * (1.0 / LEVELS), 0.0), axis=1, keepdims=True)
    return code, step


def decode(code, step, eye):
    column = jnp.sum(jnp.where(eye[None], step, 0.0), axis=2, keepdims=True)
    return code.astype(jnp.int32).astype(jnp.float32) * column


def greet(me, n, rounds=()):
    barrier = pltpu.get_barrier_semaphore()
    for axis, bit in rounds:
        pl.semaphore_signal(barrier, inc=1, device_id=partner(axis, bit), device_id_type=MESH)

    @pl.when(me > 0)
    def _():
        pl.semaphore_signal(barrier, inc=1, device_id={"blk": me - 1}, device_id_type=MESH)

    @pl.when(me < n - 1)
    def _():
        pl.semaphore_signal(barrier, inc=1, device_id={"blk": me + 1}, device_id_type=MESH)

    peers = jnp.where(me > 0, 1, 0) + jnp.where(me < n - 1, 1, 0)
    pl.semaphore_wait(barrier, peers + len(rounds))


def gather_steps(me, n, base, count, size, own_ref, slab_ref, send_sem, recv_sem):
    blocks = own_ref.shape[0]
    pieces = count // size

    def copy(way, t, c, owner):
        here = slab_ref.at[pl.ds(owner * blocks + base + c * size, size)]
        return pltpu.make_async_remote_copy(
            src_ref=here,
            dst_ref=here,
            send_sem=send_sem.at[way, t, c],
            recv_sem=recv_sem.at[way, t, c],
            device_id={"blk": me + 1 - 2 * way},
            device_id_type=MESH,
        )

    def first(way, c):
        return pltpu.make_async_remote_copy(
            src_ref=own_ref.at[pl.ds(base + c * size, size)],
            dst_ref=slab_ref.at[pl.ds(me * blocks + base + c * size, size)],
            send_sem=send_sem.at[way, 0, c],
            recv_sem=recv_sem.at[way, 0, c],
            device_id={"blk": me + 1 - 2 * way},
            device_id_type=MESH,
        )

    def has(way, t):
        behind = me if way == 0 else n - 1 - me
        return behind >= t

    def goes(way):
        return me < n - 1 if way == 0 else me > 0

    def owner_of(way, t):
        return me - t if way == 0 else me + t

    def step(v):
        t = v // pieces
        c = v % pieces
        for way in (0, 1):

            @pl.when((t == 0) & goes(way))
            def _(way=way):
                first(way, c).start()

            @pl.when((t > 0) & has(way, t))
            def _(way=way):
                copy(way, t - 1, c, owner_of(way, t)).wait_recv()

            @pl.when((t > 0) & (t < n - 1) & has(way, t) & goes(way))
            def _(way=way):
                copy(way, t, c, owner_of(way, t)).start()

    def finish():
        @pl.loop(0, (n - 1) * pieces)
        def _(v):
            t = v // pieces
            c = v % pieces
            for way in (0, 1):

                @pl.when(has(way, t) & goes(way))
                def _(way=way):
                    copy(way, t, c, me).wait_send()

    return step, n * pieces, finish


def gather_sems(n, count, size):
    return [pltpu.SemaphoreType.DMA((2, n - 1, count // size))] * 2


def gather(omega, n, parts):
    blocks, side, width = omega.shape
    wide = width // parts
    size = divisor(blocks, 4)
    pieces = blocks // size

    def body(omega_ref, *refs):
        slab_ref, *own_refs = refs[: 1 + parts]
        raw, turned, raw_sem, own_sem, *sems = refs[1 + parts :]
        me = lax.axis_index("blk")

        def load(c):
            at = pl.ds(c * size, size)
            return pltpu.make_async_copy(omega_ref.at[at], raw.at[at], raw_sem.at[c])

        def keep(p, c):
            at = pl.ds(c * size, size)
            return pltpu.make_async_copy(turned.at[p, at], own_refs[p].at[at], own_sem.at[p, c])

        for c in range(pieces):
            load(c).start()
        greet(me, n)
        step, steps, finish = gather_steps(me, n, 0, blocks, size, turned.at[0], slab_ref, *sems)

        @pl.loop(0, steps)
        def _(s):
            @pl.when(s < pieces)
            def _():
                load(s).wait()
                for i in range(size):
                    block = raw[s * size + i].T
                    for p in range(parts):
                        turned[p, s * size + i] = block[p * wide : (p + 1) * wide]

            step(s)

            @pl.when(s < pieces)
            def _():
                for p in range(parts):
                    keep(p, s).start()

        finish()

        @pl.loop(0, pieces)
        def _(c):
            for p in range(parts):
                keep(p, c).wait()

    return pl.pallas_call(
        body,
        out_shape=[jax.ShapeDtypeStruct((n * blocks, wide, side), omega.dtype)]
        + [jax.ShapeDtypeStruct((blocks, wide, side), omega.dtype)] * parts,
        in_specs=[ANY],
        out_specs=[ANY] * (1 + parts),
        scratch_shapes=[
            pltpu.VMEM(omega.shape, omega.dtype),
            pltpu.VMEM((parts, blocks, wide, side), omega.dtype),
            pltpu.SemaphoreType.DMA((pieces,)),
            pltpu.SemaphoreType.DMA((parts, pieces)),
        ]
        + gather_sems(n, blocks, size),
        compiler_params=pltpu.CompilerParams(collective_id=1, has_side_effects=True),
        name="gather",
    )(omega)


def reduce_scratch(n, count, size, wide, side, lanes):
    far = (n - 1) * count
    sems = pltpu.SemaphoreType.DMA((2, 2, far // size))
    code = pltpu.VMEM((2, far, wide, side), jnp.int16)
    step = pltpu.VMEM((2, far // size, 1, lanes), jnp.float32)
    return [code, step, code, step, sems, sems]


def reduce_steps(me, n, count, size, eye, read, total, base, scratch, beside, start):
    in_code, in_step, out_code, out_step, send_sem, recv_sem = scratch
    pieces = count // size
    reach = (n - 1) * pieces
    far = ((n - 1 - me) * pieces, me * pieces)
    hop = max(pieces, HOP) if beside else HOP

    def copies(way, u):
        to = {"blk": me + 1 - 2 * way}
        pairs = (out_code, in_code, pl.ds(u * size, size)), (out_step, in_step, pl.ds(u, 1))
        return [
            pltpu.make_async_remote_copy(
                src_ref=src.at[way, here],
                dst_ref=dst.at[way, here],
                send_sem=send_sem.at[way, kind, u],
                recv_sem=recv_sem.at[way, kind, u],
                device_id=to,
                device_id_type=MESH,
            )
            for kind, (src, dst, here) in enumerate(pairs)
        ]

    def incoming(way, u):
        return decode(in_code[way, pl.ds(u * size, size)], in_step[way, pl.ds(u, 1)], eye)

    def push(way, u, value):
        code, step = encode(value, eye)
        out_code[way, pl.ds(u * size, size)] = code
        out_step[way, pl.ds(u, 1)] = step
        for one in copies(way, u):
            one.start()

    def source(way, u):
        d = n - 1 - u // pieces if way == 0 else u // pieces
        return read(d, u % pieces)

    def step(s):
        for way in (0, 1):
            behind = me if way == 0 else n - 1 - me
            u = s - start - hop * behind
            inside = (u >= 0) & (u < far[way])

            @pl.when(inside & (behind == 0))
            def _(way=way, u=u):
                push(way, u, source(way, u))

            @pl.when(inside & (behind > 0))
            def _(way=way, u=u):
                for one in copies(way, u):
                    one.wait_recv()
                push(way, u, source(way, u) + incoming(way, u))

            @pl.when((behind > 0) & (u >= far[way]) & (u < far[way] + pieces))
            def _(way=way, u=u):
                for one in copies(way, u):
                    one.wait_recv()
                at = pl.ds(base + (u - far[way]) * size, size)
                total[at] = total[at] + incoming(way, u)

    def finish():
        @pl.loop(0, reach)
        def _(u):
            for way in (0, 1):

                @pl.when(u < far[way])
                def _(way=way):
                    for one in copies(way, u):
                        one.wait_send()

    return step, start + max([reach] + [hop * b + (n - b) * pieces for b in range(1, n)]), finish


def halves(x):
    high = x.astype(jnp.bfloat16)
    return high, (x - high.astype(jnp.float32)).astype(jnp.bfloat16)


def outer(x, y):
    return lax.dot_general(x, y, (((1,), (1,)), ((), ())), preferred_element_type=jnp.float32)


def exact(x, y, a, b):
    return lax.dot_general(
        x,
        y,
        (((a,), (b,)), ((), ())),
        precision=lax.Precision.HIGHEST,
        preferred_element_type=jnp.float32,
    )


def rounds_of():
    rounds = []
    for axis in ("row", "blk"):
        size = lax.axis_size(axis)
        assert size & (size - 1) == 0
        rounds += [(axis, 1 << b) for b in range(size.bit_length() - 1)]
    return rounds


def partner(axis, bit):
    at = lax.axis_index(axis)
    return {axis: at + bit * (1 - 2 * (at // bit % 2))}


def exchange(i, axis, bit, sums, landed, send_sem, recv_sem):
    return pltpu.make_async_remote_copy(
        src_ref=sums.at[i],
        dst_ref=landed.at[i],
        send_sem=send_sem.at[i],
        recv_sem=recv_sem.at[i],
        device_id=partner(axis, bit),
        device_id_type=MESH,
    )


def eliminate(left, right):
    height, width = left.shape
    panel = divisor(height, 8)
    down = lax.broadcasted_iota(jnp.int32, (panel, width), 0)
    over = lax.broadcasted_iota(jnp.int32, (panel, width), 1)

    def step(q):
        first = pl.multiple_of(q * panel, panel)
        here = pl.ds(first, panel)
        rows = [left[here], right[here]]
        columns = [
            jnp.broadcast_to(
                jnp.sum(jnp.where(over == first + t, rows[0], 0.0), axis=1, keepdims=True),
                (panel, width),
            )
            for t in range(panel)
        ]
        for t in range(panel):
            scale = 1.0 / jnp.sqrt(columns[t][t : t + 1])
            factors = jnp.where(down > t, columns[t] * scale, 0.0)

            def pass_on(x, t=t, scale=scale, factors=factors):
                row = x[t : t + 1] * scale
                return jnp.where(down == t, row, x - factors * row)

            columns = [pass_on(x) if u > t else x for u, x in enumerate(columns)]
            rows = [pass_on(x) for x in rows]
        below = jnp.where(over >= first + panel, rows[0], 0.0)
        left[here] = rows[0]
        right[here] = rows[1]
        left[...] = left[...] - exact(below, rows[0], 0, 0)[:height]
        right[...] = right[...] - exact(below, rows[1], 0, 0)[:height]

    return step, height // panel


def known_gram(g, sources, now_size, now, half, wide, side, width, total_rows, mine, rounds, final):
    q = len(sources[0])
    known = q * wide
    chunks = now // now_size
    early_chunks = half // now_size
    buffer, total, sums, landed = g["zbuf"], g["total"], g["gram_sums"], g["gram_landed"]
    left, right = g["left"], g["right"]
    tail_sums, tail_landed, cross = g["tail_sums"], g["tail_landed"], g["tail_sums"].at[0]
    f32 = jnp.float32

    def load(c, p, late):
        at = (c - early_chunks if late else c) * now_size
        return pltpu.make_async_copy(
            sources[1 if late else 0][p].at[pl.ds(at, now_size)],
            buffer.at[c % 2, p],
            g["zbuf_sem"].at[c % 2, p],
        )

    def fetch(c):
        for late in (False, True):

            @pl.when((c >= early_chunks) == late)
            def _(late=late):
                for p in range(q):
                    load(c, p, late).start()

    def ready(c):
        for p in range(q):
            pltpu.make_async_copy(
                sources[0][p].at[pl.ds(0, now_size)], buffer.at[c % 2, p], g["zbuf_sem"].at[c % 2, p]
            ).wait()

    def follow(c):
        @pl.when(c + 1 < chunks)
        def _():
            fetch(c + 1)

        ready(c)

    def inner(c):
        follow(c)
        part = None
        blank = jnp.zeros((width - known, side), jnp.bfloat16)
        for b in range(now_size):
            z = jnp.concatenate([buffer[c % 2, p, b] for p in range(q)], axis=0)
            high, low = halves(z)
            term = outer(
                jnp.concatenate([high, low], axis=0), jnp.concatenate([high, blank], axis=0)
            )
            part = term if part is None else part + term
        total[...] += part

    def rows_of(c):
        follow(c)
        part = None
        for b in range(now_size):
            z = [buffer[c % 2, p, b] for p in range(q)] + [mine[c * now_size + b]]
            high, low = halves(jnp.concatenate(z, axis=0))
            both = outer(jnp.concatenate([high[known:], low[known:]], axis=0), high)
            term = both[:wide] + both[wide:] + outer(high[known:], low)
            part = term if part is None else part + term
        cross[...] += part

    count = len(rounds)
    panel_step, panels = eliminate(left, right)
    per_tick = 3
    solved = chunks + count + 1
    start = max(final, solved + -(-panels // per_tick))

    def begin():
        total[...] = jnp.zeros((2 * known, width), f32)
        cross[...] = jnp.zeros((wide, width), f32)
        fetch(0)

    def copy(i):
        return exchange(i, *rounds[i], sums, landed, g["gram_send"], g["gram_recv"])

    def step(s):
        @pl.when(s < chunks)
        def _():
            inner(s)

        for i in range(count + 1):

            @pl.when(s == chunks + i)
            def _(i=i):
                if i == 0:
                    low = total[known:]
                    square = jnp.concatenate([low, jnp.zeros((width - known, width), f32)], axis=0)
                    sums[0] = total[:known] + (low + square.T[:known])
                else:
                    copy(i - 1).wait()
                    sums[i] = sums[i - 1] + landed[i - 1]
                if i < count:
                    copy(i).start()
                else:
                    across = lax.broadcasted_iota(jnp.int32, (known, width), 0)
                    along = lax.broadcasted_iota(jnp.int32, (known, width), 1)
                    left[...] = sums[count] / total_rows
                    right[...] = jnp.where(across == along, 1.0, 0.0)

        for j in range(per_tick):
            panel = (s - solved) * per_tick + j

            @pl.when((s >= solved) & (panel < panels))
            def _(panel=panel):
                panel_step(panel)

        @pl.when(s == start - 1)
        def _():
            fetch(0)

        @pl.when(s >= start)
        def _():
            rows_of(s - start)

    def end():
        upper, inverse, corner_left, corner_right = (
            g[k] for k in ("upper_ref", "inverse_ref", "corner_left", "corner_right")
        )
        for i, (axis, bit) in enumerate(rounds):
            copy = exchange(i, axis, bit, tail_sums, tail_landed, g["tail_send"], g["tail_recv"])
            copy.start()
            if i == 0:
                across = lax.broadcasted_iota(jnp.int32, (known, width), 0)
                along = lax.broadcasted_iota(jnp.int32, (known, width), 1)
                blank = jnp.zeros((width - known, width), f32)
                upper[:known] = jnp.where(along >= across, left[...], 0.0)
                inverse[:known] = jnp.where(along <= across, right[...], 0.0)
                upper[known:] = blank
                inverse[known:] = blank
            copy.wait()
            tail_sums[i + 1] = tail_sums[i] + tail_landed[i]
        mixed = tail_sums[count] / total_rows
        head = inverse[...]
        turned = exact(mixed, head, 1, 1)
        corner_left[...] = mixed[:, known:] - exact(turned, turned, 1, 1)
        across = lax.broadcasted_iota(jnp.int32, (wide, wide), 0)
        along = lax.broadcasted_iota(jnp.int32, (wide, wide), 1)
        corner_right[...] = jnp.where(across == along, 1.0, 0.0)
        corner_step, corner_panels = eliminate(corner_left, corner_right)
        pl.loop(0, corner_panels)(corner_step)
        last_inverse = jnp.where(along <= across, corner_right[...], 0.0)
        upper[:known, known:] = turned.T[:known]
        upper[known:, known:] = jnp.where(along >= across, corner_left[...], 0.0)
        inverse[known:, :] = -exact(last_inverse, exact(turned, head, 1, 0), 1, 0)
        inverse[known:, known:] = last_inverse

    return begin, step, start + chunks, end


def stage(part, values, own, slab, tables, n, following=None, rest=None, sources=None, total_rows=0):
    rows, per, side, _ = values.shape
    blocks, wide, _ = own.shape
    lanes = 128
    items = rows * per
    columns = n * blocks
    batch = divisor(rows, 4)
    pieces = rows // batch
    lag = HOP * (n - 1)
    slots = lag + 2
    half = blocks // 2
    late = blocks - half
    now = half if following is not None else blocks
    now_size = divisor(now, 4) if following is not None else divisor(math.gcd(half, late), 8)
    rounds = rounds_of() if following is None else []
    late_size = divisor(late, 4)
    gather_size = divisor(half, 4)
    f32 = jnp.float32

    args = dict(zip(("cols", "weights", "prev", "last"), tables))
    args.update(values=values, own=own, slab=slab)
    specs = [SMEM] * 4 + [ANY] * 3
    cuts = [(0, half)] + ([(half, blocks)] if following is None else [])
    outs = {
        f"piece{i}": jax.ShapeDtypeStruct((b - a, wide, side), f32) for i, (a, b) in enumerate(cuts)
    }
    scratch = dict(
        held=pltpu.VMEM((columns, wide, side), own.dtype),
        ring=pltpu.VMEM((slots, batch, per, side, side), values.dtype),
        part=pltpu.VMEM((rows, wide, side), f32),
        in_code=pltpu.VMEM((2, rows, wide, side), jnp.int16),
        in_step=pltpu.VMEM((2, pieces, 1, lanes), f32),
        out_code=pltpu.VMEM((2, rows, wide, side), jnp.int16),
        out_step=pltpu.VMEM((2, pieces, 1, lanes), f32),
        sums=pltpu.VMEM((items + 1, wide, side), f32),
        mine=pltpu.VMEM((now, wide, side), f32),
        held_sem=pltpu.SemaphoreType.DMA((n,)),
        ring_sem=pltpu.SemaphoreType.DMA((slots,)),
        send_sem=pltpu.SemaphoreType.DMA((2, 2, pieces)),
        recv_sem=pltpu.SemaphoreType.DMA((2, 2, pieces)),
        mine_sem=pltpu.SemaphoreType.DMA((len(cuts),)),
    )

    def group(name, shapes):
        scratch.update({f"{name}{i}": shape for i, shape in enumerate(shapes)})
        return [f"{name}{i}" for i in range(len(shapes))]

    now_names = group("now", reduce_scratch(n, now, now_size, wide, side, lanes))
    if following is not None:
        args.update(following=following)
        specs.append(ANY)
        outs.update(
            following_slab=jax.ShapeDtypeStruct(slab.shape, slab.dtype),
            rest_out=jax.ShapeDtypeStruct((n * late, wide, side), f32),
        )
        early_names = group("early", gather_sems(n, half, gather_size))
        after_names = group("after", gather_sems(n, late, late_size))
        scratch.update(
            shelf=pltpu.VMEM((2, late_size, wide, side), f32),
            shelf_sem=pltpu.SemaphoreType.DMA((2,)),
        )
    if rest is not None:
        args.update(rest=rest)
        specs.append(ANY)
        outs.update(rest_piece=jax.ShapeDtypeStruct((late, wide, side), f32))
        late_names = group("late", reduce_scratch(n, late, late_size, wide, side, lanes))
        scratch.update(
            zs=pltpu.VMEM((n * late, wide, side), f32),
            zs_sem=pltpu.SemaphoreType.DMA(()),
        )
    out_specs = [ANY] * len(outs)
    if following is None:
        q = (len(sources) + 1) // 2
        known, width = q * wide, (q + 1) * wide
        args.update({f"source{i}": x for i, x in enumerate(sources)})
        specs += [ANY] * len(sources)
        square = jax.ShapeDtypeStruct((width, width), f32)
        outs.update(upper=square, inverse=square)
        out_specs += [pl.BlockSpec(memory_space=pltpu.VMEM)] * 2
        scratch.update(
            zbuf=pltpu.VMEM((2, q, now_size, wide, side), f32),
            zbuf_sem=pltpu.SemaphoreType.DMA((2, q)),
            total=pltpu.VMEM((2 * known, width), f32),
            gram_sums=pltpu.VMEM((len(rounds) + 1, known, width), f32),
            gram_landed=pltpu.VMEM((len(rounds), known, width), f32),
            left=pltpu.VMEM((known, width), f32),
            right=pltpu.VMEM((known, width), f32),
            tail_sums=pltpu.VMEM((len(rounds) + 1, wide, width), f32),
            tail_landed=pltpu.VMEM((len(rounds), wide, width), f32),
            corner_left=pltpu.VMEM((wide, wide), f32),
            corner_right=pltpu.VMEM((wide, wide), f32),
            tail_send=pltpu.SemaphoreType.DMA((len(rounds),)),
            tail_recv=pltpu.SemaphoreType.DMA((len(rounds),)),
            gram_send=pltpu.SemaphoreType.DMA((len(rounds),)),
            gram_recv=pltpu.SemaphoreType.DMA((len(rounds),)),
        )
    names = list(args) + list(outs) + list(scratch)
    names[len(args) : len(args) + len(outs)] = [f"{name}_ref" for name in outs]
    names[: len(args)] = [f"{name}_ref" for name in args]

    def body(*refs):
        g = dict(zip(names, refs, strict=True))
        cols_ref, weights_ref, prev_ref, last_ref = (
            g[k] for k in ("cols_ref", "weights_ref", "prev_ref", "last_ref")
        )
        held, ring, part_ref, sums = g["held"], g["ring"], g["part"], g["sums"]
        in_code, in_step, out_code, out_step = (
            g[k] for k in ("in_code", "in_step", "out_code", "out_step")
        )
        me = lax.axis_index("blk")
        eye = diagonal(wide, lanes)

        def load(c):
            slot = c % slots
            return pltpu.make_async_copy(
                g["values_ref"].at[pl.ds(c * batch, batch)], ring.at[slot], g["ring_sem"].at[slot]
            )

        def shard(d, src):
            return pltpu.make_async_copy(
                src, held.at[pl.ds(d * blocks, blocks)], g["held_sem"].at[d]
            )

        load(0).start()
        for d in range(n):

            @pl.when(me == d)
            def _(d=d):
                shard(d, g["own_ref"]).start()

            @pl.when(me != d)
            def _(d=d):
                shard(d, g["slab_ref"].at[pl.ds(d * blocks, blocks)]).start()

        if rest is not None:
            zs_copy = pltpu.make_async_copy(g["rest_ref"], g["zs"], g["zs_sem"])
            zs_copy.start()
        greet(me, n, rounds)
        sums[items] = jnp.zeros((wide, side), f32)

        @pl.when(me == 0)
        def _():
            in_step[0] = jnp.zeros((pieces, 1, lanes), f32)

        @pl.when(me == n - 1)
        def _():
            in_step[1] = jnp.zeros((pieces, 1, lanes), f32)

        extra = []
        ends = []
        if following is not None:
            step, steps, finish = gather_steps(
                me, n, 0, half, gather_size, g["following_ref"], g["following_slab_ref"],
                *(g[k] for k in early_names),
            )
            lead = min(LEAD, half // gather_size)
            extra.append((lambda s, step=step: step(s + lead), steps - lead))
            ends.append(finish)
            for v in range(lead):
                step(v)
        if rest is not None:
            zs = g["zs"]

            def read_rest(d, c):
                return zs[pl.ds(d * late + c * late_size, late_size)]

            step, steps, finish = reduce_steps(
                me, n, late, late_size, eye, read_rest, zs, me * late,
                [g[k] for k in late_names], following is not None,
                max(half // gather_size - LEAD, 0) if following is not None else 0,
            )
            extra.append((step, steps))
            ends.append(finish)
            zs_copy.wait()

        for d in range(n):
            shard(d, g["own_ref"]).wait()

        def copies(way, c):
            to = {"blk": me + 1 - 2 * way}
            pairs = (
                (out_code, in_code, pl.ds(c * batch, batch)),
                (out_step, in_step, pl.ds(c, 1)),
            )
            return [
                pltpu.make_async_remote_copy(
                    src_ref=src.at[way, here],
                    dst_ref=dst.at[way, here],
                    send_sem=g["send_sem"].at[way, kind, c],
                    recv_sem=g["recv_sem"].at[way, kind, c],
                    device_id=to,
                    device_id_type=MESH,
                )
                for kind, (src, dst, here) in enumerate(pairs)
            ]

        def incoming(way, c):
            code = in_code[way, pl.ds(c * batch, batch)]
            return decode(code, in_step[way, pl.ds(c, 1)], eye)

        def relay(way, c, has, goes):
            @pl.when((c >= 0) & (c < pieces) & has)
            def _():
                for one in copies(way, c):
                    one.wait_recv()

            @pl.when((c >= 0) & (c < pieces) & goes)
            def _():
                at = pl.ds(c * batch, batch)
                code, step = encode(part_ref[at] + incoming(way, c), eye)
                out_code[way, at] = code
                out_step[way, pl.ds(c, 1)] = step
                for one in copies(way, c):
                    one.start()

        first_steps = max([pieces + lag] + [steps for _, steps in extra])
        if following is not None:
            late_step, late_steps, finish = gather_steps(
                me, n, half, late, late_size, g["following_ref"], g["following_slab_ref"],
                *(g[k] for k in after_names),
            )
            ends.append(finish)
            ahead = late // late_size

        @pl.loop(0, first_steps)
        def _(s):
            @pl.when(s + 1 < pieces)
            def _():
                load(s + 1).start()

            @pl.when(s < pieces)
            def _():
                load(s).wait()
                for r in range(batch):
                    total = None
                    for k in range(per):
                        at = (s * batch + r) * per + k
                        term = weights_ref[at] * lax.dot_general(
                            held[cols_ref[at]],
                            ring[s % slots, r, k],
                            (((1,), (1,)), ((), ())),
                            preferred_element_type=f32,
                        )
                        total = term if total is None else total + term
                    part_ref[s * batch + r] = total

            relay(0, s - HOP * me, me > 0, me < n - 1)
            relay(1, s - HOP * (n - 1 - me), me < n - 1, me > 0)
            for step, steps in extra:

                @pl.when(s < steps)
                def _(step=step):
                    step(s)

            if following is not None:

                @pl.when(s >= first_steps - ahead)
                def _():
                    late_step(s - (first_steps - ahead))

            c = s - lag

            @pl.when((c >= 0) & (c < pieces))
            def _():
                total = part_ref[pl.ds(c * batch, batch)] + incoming(0, c) + incoming(1, c)
                high = total.astype(jnp.bfloat16)
                low = (total - high.astype(f32)).astype(jnp.bfloat16)
                for r in range(batch):
                    both = jnp.concatenate([high[r], low[r]], axis=0)
                    for k in range(per):
                        at = (c * batch + r) * per + k
                        pair = lax.dot_general(
                            both,
                            ring[c % slots, r, k],
                            (((1,), (0,)), ((), ())),
                            preferred_element_type=f32,
                        )
                        term = weights_ref[at] * (pair[:wide] + pair[wide:])
                        sums[at] = term + sums[prev_ref[at]]

        if rest is not None:
            rest_copy = pltpu.make_async_copy(
                g["zs"].at[pl.ds(me * late, late)], g["rest_piece_ref"], g["zs_sem"]
            )
            rest_copy.start()

        mine = g["mine"]

        @pl.loop(0, now)
        def _(i):
            mine[i] = sums[last_ref[me * blocks + i]]

        def read_now(d, c):
            first = d * blocks + c * now_size
            return jnp.stack([sums[last_ref[first + i]] for i in range(now_size)])

        step, steps, finish = reduce_steps(
            me, n, now, now_size, eye, read_now, mine, 0, [g[k] for k in now_names],
            following is not None, 0,
        )
        second = [(step, steps)]
        ends.append(finish)
        if following is None:
            rest_copy.wait()
            early = [g[f"source{2 * i}_ref"] for i in range(q)]
            late_refs = [g[f"source{2 * i + 1}_ref"] for i in range(q - 1)]
            late_refs.append(g["rest_piece_ref"])
            share = now // now_size
            begin, step, steps, close = known_gram(
                g, (early, late_refs), now_size, now, half, wide, side, width, total_rows, mine,
                rounds, max(HOP + (n - 2) * share, HOP * (n - 1)),
            )
            begin()
            second.append((step, steps))
        if following is not None:
            second.append((lambda s: late_step(s + ahead), late_steps - ahead))
            shelf = g["shelf"]
            shelves = n * late // late_size
            per_shard = late // late_size

            def store(i):
                return pltpu.make_async_copy(
                    shelf.at[i % 2],
                    g["rest_out_ref"].at[pl.ds(i * late_size, late_size)],
                    g["shelf_sem"].at[i % 2],
                )

            def keep(i):
                @pl.when(i >= 2)
                def _():
                    store(i - 2).wait()

                first = i // per_shard * blocks + half + i % per_shard * late_size
                for j in range(late_size):
                    shelf[i % 2, j] = sums[last_ref[first + j]]
                store(i).start()

            second.append((keep, shelves))

        @pl.loop(0, max(steps for _, steps in second))
        def _(s):
            for step, steps in second:

                @pl.when(s < steps)
                def _(step=step):
                    step(s)

        mine_copies = [
            pltpu.make_async_copy(
                mine.at[pl.ds(a, b - a)], g[f"piece{i}_ref"], g["mine_sem"].at[i]
            )
            for i, (a, b) in enumerate(cuts)
        ]
        for one in mine_copies:
            one.start()
        if following is None:
            close()

        @pl.loop(0, pieces)
        def _(c):
            @pl.when(me < n - 1)
            def _():
                for one in copies(0, c):
                    one.wait_send()

            @pl.when(me > 0)
            def _():
                for one in copies(1, c):
                    one.wait_send()

        for finish in ends:
            finish()
        if following is not None:
            for i in range(max(shelves - 2, 0), shelves):
                store(i).wait()
        if rest is not None and following is not None:
            rest_copy.wait()
        for one in mine_copies:
            one.wait()

    results = pl.pallas_call(
        body,
        out_shape=list(outs.values()),
        in_specs=specs,
        out_specs=out_specs,
        scratch_shapes=list(scratch.values()),
        compiler_params=pltpu.CompilerParams(
            collective_id=2 + part, has_side_effects=True, vmem_limit_bytes=63 << 20
        ),
        name=f"stage_{part}",
    )(*args.values())
    return dict(zip(outs, results))


def join(z_refs, early, b):
    here = [z_refs[2 * p + (0 if early else 1)][b] for p in range(len(z_refs) // 2)]
    return jnp.concatenate(here, axis=0)


def block_specs(pieces, batch, early_steps):
    specs = []
    for i, piece in enumerate(pieces):
        shape = (batch,) + piece.shape[1:]
        if i % 2 == 0:
            specs.append(pl.BlockSpec(shape, lambda i: (jnp.minimum(i, early_steps - 1), 0, 0)))
        else:
            specs.append(pl.BlockSpec(shape, lambda i: (jnp.maximum(i - early_steps, 0), 0, 0)))
    return specs


def crossed(x, y):
    return lax.dot_general(x, y, (((0,), (1,)), ((), ())), preferred_element_type=jnp.float32)


def solve(pieces, inverse):
    early, late = pieces[0].shape[0], pieces[1].shape[0]
    side = pieces[0].shape[2]
    width = sum(piece.shape[1] for piece in pieces[::2])
    batch = divisor(math.gcd(early, late), 8)

    def body(*refs):
        *z_refs, inverse_ref, out_ref = refs
        inv_high, inv_low = halves(inverse_ref[...])
        inv_twice = jnp.concatenate([inv_high, inv_high], axis=1)
        for first in (True, False):

            @pl.when((pl.program_id(0) < early // batch) == first)
            def _(first=first):
                z = jnp.concatenate([join(z_refs, first, b) for b in range(batch)], axis=1)
                high, low = halves(z)
                both = jnp.concatenate([high, low], axis=0)
                out = crossed(both, inv_twice) + crossed(high, inv_low)
                out_ref[...] = out.reshape(batch, side, width)

    return pl.pallas_call(
        body,
        out_shape=jax.ShapeDtypeStruct((early + late, side, width), jnp.float32),
        grid=((early + late) // batch,),
        in_specs=block_specs(pieces, batch, early // batch)
        + [pl.BlockSpec((width, width), lambda i: (0, 0))],
        out_specs=pl.BlockSpec((batch, side, width), lambda i: (i, 0, 0)),
        name="solve",
    )(*pieces, inverse)


def local(values, scales, pattern, omega):
    rows, per = pattern.shape
    blocks, side, width = omega.shape
    n = lax.axis_size("blk")
    items = rows * per
    columns = blocks * n
    cols = pattern.reshape(-1) - lax.axis_index("row") * columns
    weights = scales.astype(jnp.float32).reshape(-1)
    slot = jnp.arange(items)
    same = cols[:, None] == cols[None, :]
    prev = jnp.max(jnp.where(same & (slot[None, :] < slot[:, None]), slot[None, :], -1), axis=1)
    prev = jnp.where(prev < 0, items, prev)
    hits = jnp.arange(columns)[:, None] == cols[None, :]
    last = jnp.max(jnp.where(hits, slot[None, :], -1), axis=1)
    last = jnp.where(last < 0, items, last)

    parts = 4
    total_rows = columns * side * lax.axis_size("row")
    slab, *own = gather(omega, n, parts)
    rest = None
    pieces = []
    for p in range(parts):
        following = own[p + 1] if p + 1 < parts else None
        done = stage(
            p, values, own[p], slab, (cols, weights, prev, last), n, following, rest,
            pieces if following is None else None, total_rows,
        )
        if p:
            pieces.append(done["rest_piece"])
        if p + 1 < parts:
            pieces.append(done["piece0"])
            slab, rest = done["following_slab"], done["rest_out"]
        else:
            pieces += [done["piece0"], done["piece1"]]

    return solve(pieces, done["inverse"]), done["upper"]


def solution(mesh):
    return jax.shard_map(
        local,
        mesh=mesh,
        in_specs=(
            P("row", "blk", None, None),
            P("row", "blk"),
            P("row", "blk"),
            P(("row", "blk"), None, None),
        ),
        out_specs=(P(("row", "blk"), None, None), P()),
        check_vma=False,
    )
```
